512 devices in a mesh: row: 32 (over x, y, core), col: 16 (over z).
Axes of the slice: x: 4, y: 4, z: 16, core: 2. Of those that a mesh axis runs over, the one named last changes fastest.
Arguments:
- features: bfloat16 [65536, 256], P('col', 'row'), may hold values from -6 to 6
- weight: bfloat16 [256, 256], replicated, may hold values from -0.375 to 0.375
- adj_values: bfloat16 [32, 16, 96, 128, 128], P('row', 'col'), may hold values from -0.0625 to 0.0625
- block_rows: int32 [32, 16, 96], P('row', 'col'), may hold values from 0 to 15, as said below
- block_cols: int32 [32, 16, 96], P('row', 'col'), may hold values from 0 to 31
- block_counts: int32 [32, 16], P('row', 'col'), may hold values from 1 to 96, as said below
- cotangent: bfloat16 [65536, 256], P(('row', 'col')), may hold values from -6 to 6
Outputs:
- output: bfloat16 [65536, 256], P(('row', 'col'))
- grad_weight: float32 [256, 256], replicated
- grad_features: bfloat16 [65536, 256], P('col', 'row')
The draws below stay inside these ranges and needn't reach their ends.
Inputs may be any that keep to these rules, and one draw needn't show every extreme that they name: Within one tile the pairs (block_rows, block_cols) over all 96 slots are distinct. `block_counts`: some tile holds exactly 96 live blocks and some other tile exactly one in every draw.
All inputs are finite; a program needn't handle non-finite values.
Results may differ from the reference program's by a relative error of at most 0.029.
Values may be sent and summed in bfloat16 or wider, within the bound.
A program may use at most 64 MiB of HBM per device.

```python
import math
import jax
import jax.numpy as jnp
from jax import lax

F = 256
BLK = 128
RB = 16
CB = 32
MAXB = 96
NODES = 65536
N_ROW = 32
N_COL = 16


def tile_slots(key):
    base_key = jax.random.fold_in(key, 7)
    tile_keys = jax.random.split(base_key, N_ROW * N_COL)
    orders = jax.vmap(lambda tile_key: jax.random.permutation(tile_key, RB * CB))(tile_keys)
    return orders[:, :MAXB].reshape(N_ROW, N_COL, MAXB).astype(jnp.int32)


def draw_block_rows(key, part):
    return (tile_slots(key) // CB).astype(jnp.int32)


def draw_block_cols(key, part):
    return (tile_slots(key) % CB).astype(jnp.int32)


def draw_block_counts(key, part):
    first_key, second_key, third_key, fourth_key = jax.random.split(jax.random.fold_in(key, 11), 4)
    levels = jax.random.randint(first_key, (N_ROW, 1), MAXB // 4, MAXB + 1, dtype=jnp.int32)
    jitter = jax.random.randint(second_key, (N_ROW, N_COL), 0, MAXB // 8 + 1, dtype=jnp.int32)
    counts = jnp.maximum(levels - jitter, 1)
    total_tiles = N_ROW * N_COL
    chosen = jax.random.randint(third_key, (), 0, total_tiles, dtype=jnp.int32)
    step_away = jax.random.randint(fourth_key, (), 1, total_tiles, dtype=jnp.int32)
    lonely = (chosen + step_away) % total_tiles
    places = jnp.arange(total_tiles, dtype=jnp.int32).reshape(N_ROW, N_COL)
    counts = jnp.where(places == lonely, 1, counts)
    return jnp.where(places == chosen, MAXB, counts).astype(jnp.int32)


def block_scale(own_key, shape, pieces, least, largest):
    level = 1.0
    for dim, shards_of in pieces:
        steps = jax.random.uniform(jax.random.fold_in(jax.random.fold_in(own_key, 6), dim), (shards_of,), jnp.float32, least / len(pieces), largest / len(pieces))
        level = level * jnp.repeat(jnp.exp(steps), shape[dim] // shards_of).reshape((-1,) + (1,) * (len(shape) - 1 - dim))
    return level


def scatter_about(stream_key, shape, scale, bound, cuts=(), held_as=jnp.bfloat16):
    entries = scale * jax.random.normal(stream_key, shape, jnp.float32)
    if cuts:
        entries = entries * block_scale(stream_key, shape, cuts, -0.22, 0.18)
    return jnp.clip(entries, -bound, bound).astype(held_as)


def setup_inputs(seed: int = 0) -> dict:
    key_of = jax.random.split(jax.random.key(seed), 8)
    return {
        "features": scatter_about(key_of[0], (NODES, F), 1.0, 6.0, ((0, 16), (1, 32))),
        "weight": scatter_about(key_of[1], (F, F), F ** -0.5, 0.375),
        "adj_values": scatter_about(key_of[2], (N_ROW, N_COL, MAXB, BLK, BLK), (5 * MAXB * N_COL * BLK // (8 * RB)) ** -0.5, 0.0625, ((0, 32), (1, 16))),
        "block_rows": draw_block_rows(jax.random.fold_in(key_of[7], 71), 0),
        "block_cols": draw_block_cols(jax.random.fold_in(key_of[7], 71), 0),
        "block_counts": draw_block_counts(jax.random.fold_in(key_of[7], 71), 0),
        "cotangent": scatter_about(key_of[6], (NODES, F), 1.0, 6.0, ((0, 512),)),
    }


def reference(features, weight, adj_values, block_rows, block_cols, block_counts, cotangent):
    is_live = (jnp.arange(MAXB, dtype=jnp.int32)[None, None, :] < block_counts[:, :, None]).astype(jnp.float32)
    panels = features.reshape(N_COL, CB, BLK, F)

    def forward_group(row_group):

        def tile(col_group):
            tile_vals = adj_values[row_group, col_group].astype(jnp.float32) * is_live[row_group, col_group][:, None, None]
            picked = panels[col_group][block_cols[row_group, col_group]].astype(jnp.float32)
            product = jnp.einsum('bij,bjf->bif', tile_vals, picked, precision=lax.Precision.HIGHEST)
            return jnp.zeros((RB, BLK, F), jnp.float32).at[block_rows[row_group, col_group]].add(product)
        return lax.optimization_barrier(jnp.sum(lax.map(tile, jnp.arange(N_COL, dtype=jnp.int32)), axis=0))
    aggregated = lax.map(forward_group, jnp.arange(N_ROW, dtype=jnp.int32)).reshape(NODES, F).astype(jnp.bfloat16)
    preact = jnp.dot(aggregated, weight, preferred_element_type=jnp.float32)
    output = jax.nn.silu(preact).astype(jnp.bfloat16)
    sigmoid_pre = jax.nn.sigmoid(preact)
    slopes = sigmoid_pre * (1.0 + preact * (1.0 - sigmoid_pre))
    deltas = (cotangent.astype(jnp.float32) * slopes).astype(jnp.bfloat16)
    grad_weight = jnp.dot(aggregated.T, deltas, preferred_element_type=jnp.float32) * (1.0 / math.sqrt(NODES))
    backward = jnp.dot(deltas, weight.T, preferred_element_type=jnp.float32).astype(jnp.bfloat16)
    back_slabs = backward.reshape(N_ROW, RB, BLK, F)

    def backward_group(col_group):

        def tile(row_group):
            tile_vals = adj_values[row_group, col_group].astype(jnp.float32) * is_live[row_group, col_group][:, None, None]
            picked = back_slabs[row_group][block_rows[row_group, col_group]].astype(jnp.float32)
            product = jnp.einsum('bij,bif->bjf', tile_vals, picked, precision=lax.Precision.HIGHEST)
            summed = jnp.zeros((CB, BLK, F), jnp.float32).at[block_cols[row_group, col_group]].add(product)
            rounded = lax.optimization_barrier(summed.astype(jnp.bfloat16))
            return rounded.astype(jnp.float32)
        return lax.optimization_barrier(jnp.sum(lax.map(tile, jnp.arange(N_ROW, dtype=jnp.int32)), axis=0))
    grad_features = lax.map(backward_group, jnp.arange(N_COL, dtype=jnp.int32)).reshape(NODES, F).astype(jnp.bfloat16)
    return (output, grad_weight, grad_features)
```

```python
import functools
import math

import jax
import jax.numpy as jnp
from jax import lax
from jax.experimental import pallas as pl
from jax.experimental.pallas import tpu as pltpu
from jax.sharding import PartitionSpec as P

MESH = pl.DeviceIdType.MESH
VMEM_LIMIT = 56 * 2**20
NT = (((1,), (1,)), ((), ()))
TN = (((0,), (0,)), ((), ()))
DMA = pltpu.SemaphoreType.DMA
BF16, F32 = jnp.bfloat16, jnp.float32


class Place:
    def __init__(self, n_row, n_col):
        self.n_row, self.n_col = n_row, n_col
        self.chips = n_row // 2
        self.side = math.isqrt(self.chips)
        self.row, self.col = lax.axis_index("row"), lax.axis_index("col")
        self.core = lax.rem(self.row, 2)
        chip = lax.div(self.row, 2)
        self.x, self.y = lax.div(chip, self.side), lax.rem(chip, self.side)

    def chip(self, k, sign=1):
        dx, dy = lax.div(k, self.side), lax.rem(k, self.side)
        x = lax.rem(self.x + sign * dx + self.side, self.side)
        y = lax.rem(self.y + sign * dy + self.side, self.side)
        return x * self.side + y

    def at(self, row=None, col=None):
        return (self.row if row is None else row, self.col if col is None else col)

    def sibling(self):
        return self.at(row=self.row + 1 - 2 * self.core)

    def peer_row(self, k):
        return lax.rem(self.row + k, self.n_row)

    def peer_col(self, k):
        return lax.rem(self.col + k + self.n_col, self.n_col)


def signal(barrier, device):
    pl.semaphore_signal(barrier, inc=1, device_id=device, device_id_type=MESH)


def remote(src, dst, send, recv, device):
    return pltpu.make_async_remote_copy(
        src_ref=src, dst_ref=dst, send_sem=send, recv_sem=recv, device_id=device, device_id_type=MESH
    )


def loop(start, stop, body):
    def step(i, carry):
        body(jnp.int32(i))
        return carry

    lax.fori_loop(start, stop, step, 0)


def gather_kernel(n_row, n_col, mine, out, send, recv, near_send, near_recv):
    at = Place(n_row, n_col)
    barrier = pltpu.get_barrier_semaphore()
    loop(1, at.chips, lambda k: signal(barrier, at.at(row=at.chip(k) * 2 + at.core)))
    signal(barrier, at.sibling())
    pl.semaphore_wait(barrier, at.chips)

    def far(k):
        return remote(mine, out.at[at.row], send.at[k], recv.at[k], at.at(row=at.chip(k) * 2 + at.core))

    def near(k):
        held = out.at[at.chip(k, -1) * 2 + at.core]
        return remote(held, held, near_send.at[k], near_recv.at[k], at.sibling())

    loop(1, at.chips, lambda k: far(k).start())
    out[at.row] = mine[...]
    near(jnp.int32(0)).start()

    def pass_on(k):
        far(k).wait_recv()
        near(k).start()

    loop(1, at.chips, pass_on)
    loop(1, at.chips, lambda k: far(k).wait_send())
    loop(0, at.chips, lambda k: near(k).wait())


def gather_rows(mine, n_row, n_col):
    chips = n_row // 2
    return pl.pallas_call(
        functools.partial(gather_kernel, n_row, n_col),
        out_shape=jax.ShapeDtypeStruct((n_row, *mine.shape), mine.dtype),
        in_specs=[pl.BlockSpec(memory_space=pltpu.VMEM)],
        out_specs=pl.BlockSpec(memory_space=pltpu.VMEM),
        scratch_shapes=[DMA((chips,))] * 4,
        compiler_params=pltpu.CompilerParams(
            collective_id=0, has_side_effects=True, vmem_limit_bytes=VMEM_LIMIT
        ),
        name="gather_rows",
    )(mine)


def product_kernel(backward, rows, cols, count, adj, panels, out, acc):
    acc[...] = jnp.zeros_like(acc)
    live = count[0]

    def product(b):
        if backward:
            value = jnp.dot(panels[rows[b]], adj[b], preferred_element_type=F32)
            return cols[b], value
        panel = panels[:, pl.ds(pl.multiple_of(cols[b] * adj.shape[2], adj.shape[2]), adj.shape[2])]
        return rows[b], lax.dot_general(adj[b], panel, NT, preferred_element_type=F32)

    def several(n, first):
        made = [product(first + i) for i in range(n)]
        for where, value in made:
            acc[where] += value

    turns = lax.div(live, 4)
    loop(0, turns, lambda t: several(4, t * 4))
    loop(turns * 4, live, lambda b: several(1, b))
    if backward:
        width = adj.shape[2]
        for c in range(acc.shape[0]):
            out[:, c * width : (c + 1) * width] = acc[c].astype(out.dtype)
    else:
        out[...] = acc[...].astype(out.dtype)


def block_product(adj, rows, cols, count, panels, blocks, backward):
    size = adj.shape[1]
    if backward:
        features = panels.shape[1]
        shape, acc = (features, blocks * size), (blocks, features, size)
    else:
        features = panels.shape[0]
        shape = acc = (blocks, size, features)
    smem, vmem = pl.BlockSpec(memory_space=pltpu.SMEM), pl.BlockSpec(memory_space=pltpu.VMEM)
    return pl.pallas_call(
        functools.partial(product_kernel, backward),
        out_shape=jax.ShapeDtypeStruct(shape, BF16),
        in_specs=[smem, smem, smem, vmem, vmem],
        out_specs=vmem,
        scratch_shapes=[pltpu.VMEM(acc, F32)],
        compiler_params=pltpu.CompilerParams(vmem_limit_bytes=VMEM_LIMIT),
        name="product_back" if backward else "product",
    )(rows, cols, count, adj, panels)


def lanes_of(n):
    return [
        (2 * way + half, 1 - 2 * way, half, n // 2 if way == half else (n - 1) // 2)
        for half in range(2)
        for way in range(2)
    ]


def middle_kernel(
    n_row, n_col, part, weight, cot, output, back, gw_part,
    ring, local, arrived, rs_send, rs_recv, ag_send, ag_recv, gw_send, gw_recv,
):
    at = Place(n_row, n_col)
    lanes = lanes_of(n_col)
    me = at.col
    most = max(steps for *_, steps in lanes)
    barrier = pltpu.get_barrier_semaphore()
    ways = [k for k in (1, n_col - 1)][: min(2, n_col - 1)]
    for k in ways:
        signal(barrier, at.at(col=at.peer_col(k)))
    loop(1, n_row, lambda k: signal(barrier, at.at(row=at.peer_row(k))))
    pl.semaphore_wait(barrier, len(ways) + n_row - 1)

    half_rows = part.shape[1] // 2

    def rs(lane, sign, s, src):
        return remote(src, ring.at[lane, s], rs_send.at[lane, s], rs_recv.at[lane, s], at.at(col=at.peer_col(sign)))

    def addend(sign, half, steps, s):
        return part.at[at.peer_col(sign * (steps - s)), pl.ds(half * half_rows, half_rows)]

    for lane, sign, half, steps in lanes:
        if steps:
            rs(lane, sign, 0, addend(sign, half, steps, 0)).start()

    def rs_step(s):
        for lane, sign, half, steps in lanes:

            @pl.when(s < steps)
            def _():
                rs(lane, sign, s - 1, ring.at[lane, s - 1]).wait_recv()
                total = ring[lane, s - 1].astype(F32) + addend(sign, half, steps, s)[...].astype(F32)
                ring[lane, s - 1] = total.astype(BF16)
                rs(lane, sign, s, ring.at[lane, s - 1]).start()

    loop(1, most, rs_step)
    halves = [part[me, h * half_rows : (h + 1) * half_rows].astype(F32) for h in range(2)]
    for lane, sign, half, steps in lanes:
        if steps:
            rs(lane, sign, steps - 1, ring.at[lane, steps - 1]).wait_recv()
            halves[half] += ring[lane, steps - 1].astype(F32)
    aggregated = jnp.concatenate(halves, axis=0).astype(BF16)

    preact = jnp.dot(aggregated, weight[...], preferred_element_type=F32)
    sigmoid = jax.nn.sigmoid(preact)
    slopes = sigmoid * (1.0 + preact * (1.0 - sigmoid))
    deltas = (cot[...].astype(F32) * slopes).astype(BF16)
    back[me] = lax.dot_general(weight[...], deltas, NT, preferred_element_type=F32).astype(BF16)

    half_back = back.shape[1] // 2

    def ag(lane, sign, half, s):
        held = back.at[at.peer_col(-sign * s), pl.ds(half * half_back, half_back)]
        return remote(held, held, ag_send.at[lane, s], ag_recv.at[lane, s], at.at(col=at.peer_col(sign)))

    def ag_wait(lane, sign, half, s):
        held = back.at[at.peer_col(-sign * (s + 1)), pl.ds(half * half_back, half_back)]
        remote(held, held, ag_send.at[lane, s], ag_recv.at[lane, s], at.at(col=at.peer_col(sign))).wait_recv()

    for lane, sign, half, steps in lanes:
        if steps:
            ag(lane, sign, half, 0).start()

    output[...] = (preact * sigmoid).astype(BF16)
    grad = lax.dot_general(aggregated, deltas, TN, preferred_element_type=F32)
    local[...] = grad.reshape(local.shape)

    def gw(k):
        return remote(local.at[at.peer_row(k)], arrived.at[k - 1], gw_send.at[k - 1], gw_recv, at.at(row=at.peer_row(k)))

    loop(1, n_row, lambda k: gw(k).start())

    def ag_step(s):
        for lane, sign, half, steps in lanes:

            @pl.when(s < steps)
            def _():
                ag_wait(lane, sign, half, s - 1)
                ag(lane, sign, half, s).start()

    loop(1, most, ag_step)
    remote(arrived, arrived, gw_send.at[0], gw_recv, at.sibling()).wait_recv()
    total = local[at.row]
    for k in range(n_row - 1):
        total += arrived[k]
    gw_part[...] = total
    for lane, sign, half, steps in lanes:
        if steps:
            ag_wait(lane, sign, half, steps - 1)
    loop(1, n_row, lambda k: gw(k).wait_send())

    def drain(s):
        for lane, sign, half, steps in lanes:

            @pl.when(s < steps)
            def _():
                rs(lane, sign, s, ring.at[lane, s]).wait_send()
                ag(lane, sign, half, s).wait_send()

    loop(0, most, drain)


def middle(part, weight, cot, n_row, n_col):
    blocks, size, features = part.shape
    steps = max(n_col // 2, 1)
    vmem = pl.BlockSpec(memory_space=pltpu.VMEM)
    ring_sems = DMA((4, steps))
    return pl.pallas_call(
        functools.partial(middle_kernel, n_row, n_col),
        out_shape=(
            jax.ShapeDtypeStruct((size, features), BF16),
            jax.ShapeDtypeStruct((blocks, features, size), BF16),
            jax.ShapeDtypeStruct((features // n_row, features), F32),
        ),
        in_specs=[vmem] * 3,
        out_specs=(vmem,) * 3,
        scratch_shapes=[
            pltpu.VMEM((4, steps, size // 2, features), BF16),
            pltpu.VMEM((n_row, features // n_row, features), F32),
            pltpu.VMEM((n_row - 1, features // n_row, features), F32),
            ring_sems, ring_sems, ring_sems, ring_sems,
            DMA((n_row - 1,)),
            DMA(()),
        ],
        compiler_params=pltpu.CompilerParams(
            collective_id=1, has_side_effects=True, vmem_limit_bytes=VMEM_LIMIT
        ),
        name="middle",
    )(part, weight, cot)


def final_kernel(
    n_row, n_col, scale, terms, gw_part, grad, gw,
    swapped, staged, arrived, z_buf, x_send, x_recv, f_send, f_recv, z_send, z_recv, g_send, g_recv,
):
    at = Place(n_row, n_col)
    barrier = pltpu.get_barrier_semaphore()
    loop(1, n_row, lambda k: signal(barrier, at.at(row=at.peer_row(k))))
    loop(1, n_col, lambda k: signal(barrier, at.at(col=at.peer_col(k))))
    pl.semaphore_wait(barrier, n_row + n_col - 2)

    def swap(k):
        return remote(terms.at[at.chip(k), 1 - at.core], swapped.at[k], x_send.at[k], x_recv.at[k], at.sibling())

    def far(k):
        return remote(
            staged.at[k], arrived.at[k - 1], f_send.at[k], f_recv.at[k], at.at(row=at.chip(k) * 2 + at.core)
        )

    def z_copy(k):
        return remote(gw_part, z_buf.at[at.col], z_send.at[k], z_recv, at.at(col=at.peer_col(k)))

    def g_copy(k):
        return remote(gw.at[at.row], gw.at[at.row], g_send.at[k], g_recv, at.at(row=at.peer_row(k)))

    loop(0, at.chips, lambda k: swap(lax.rem(k + 1, at.chips)).start())
    loop(1, n_col, lambda k: z_copy(k).start())
    z_buf[at.col] = gw_part[...]

    def add(k):
        swap(k).wait_recv()
        return terms[at.chip(k), at.core].astype(F32) + swapped[k].astype(F32)

    def add_and_send(k):
        staged[k] = add(k).astype(BF16)
        far(k).start()

    loop(1, at.chips, add_and_send)
    total = add(jnp.int32(0))
    if n_col > 1:
        most = z_buf.at[pl.ds(0, n_col - 1)]
        remote(most, most, z_send.at[0], z_recv, at.sibling()).wait_recv()
    whole = z_buf[0]
    for k in range(1, n_col):
        whole += z_buf[k]
    gw[at.row] = whole * scale
    loop(1, n_row, lambda k: g_copy(k).start())
    for k in range(1, at.chips):
        far(jnp.int32(k)).wait_recv()
        total += arrived[k - 1].astype(F32)
    grad[...] = total.astype(BF16)
    rest = gw.at[pl.ds(0, n_row - 1)]
    remote(rest, rest, g_send.at[0], g_recv, at.sibling()).wait_recv()
    loop(0, at.chips, lambda k: swap(k).wait_send())
    loop(1, at.chips, lambda k: far(k).wait_send())
    loop(1, n_col, lambda k: z_copy(k).wait_send())
    loop(1, n_row, lambda k: g_copy(k).wait_send())


def final(terms, gw_part, n_row, n_col, scale):
    chips, _, some, nodes = terms.shape
    vmem = pl.BlockSpec(memory_space=pltpu.VMEM)
    return pl.pallas_call(
        functools.partial(final_kernel, n_row, n_col, scale),
        out_shape=(
            jax.ShapeDtypeStruct((some, nodes), BF16),
            jax.ShapeDtypeStruct((n_row, *gw_part.shape), F32),
        ),
        in_specs=[vmem] * 2,
        out_specs=(vmem,) * 2,
        scratch_shapes=[
            pltpu.VMEM((chips, some, nodes), BF16),
            pltpu.VMEM((chips, some, nodes), BF16),
            pltpu.VMEM((max(chips - 1, 1), some, nodes), BF16),
            pltpu.VMEM((n_col, *gw_part.shape), F32),
            DMA((chips,)), DMA((chips,)), DMA((chips,)), DMA((chips,)),
            DMA((n_col,)), DMA(()), DMA((n_row,)), DMA(()),
        ],
        compiler_params=pltpu.CompilerParams(
            collective_id=2, has_side_effects=True, vmem_limit_bytes=VMEM_LIMIT
        ),
        name="final",
    )(terms, gw_part)


def solution(mesh):
    n_row, n_col = mesh.shape["row"], mesh.shape["col"]

    def shards(features, weight, adj_values, block_rows, block_cols, block_counts, cotangent):
        adj, rows, cols, count = adj_values[0, 0], block_rows[0, 0], block_cols[0, 0], block_counts[0]
        size = adj.shape[1]
        nodes = features.shape[0]
        width = weight.shape[0]
        panels = gather_rows(features.T, n_row, n_col).reshape(width, nodes)
        part = block_product(adj, rows, cols, count, panels, n_col, False)
        output, back, gw_part = middle(part, weight, cotangent, n_row, n_col)
        terms = block_product(adj, rows, cols, count, back, nodes // size, True)
        terms = terms.reshape(n_row // 2, 2, width // n_row, nodes)
        grad, gw = final(terms, gw_part, n_row, n_col, 1.0 / math.sqrt(nodes * n_col))
        return output, gw.reshape(width, width), grad.T

    return jax.shard_map(
        shards,
        mesh=mesh,
        in_specs=(
            P("col", "row"),
            P(),
            P("row", "col", None, None, None),
            P("row", "col", None),
            P("row", "col", None),
            P("row", "col"),
            P(("row", "col"), None),
        ),
        out_specs=(P(("row", "col"), None), P(), P("col", "row")),
        check_vma=False,
    )
```

```python
import functools
import math

import jax
import jax.numpy as jnp
from jax import lax
from jax.experimental import pallas as pl
from jax.experimental.pallas import tpu as pltpu
from jax.sharding import PartitionSpec as P

MESH = pl.DeviceIdType.MESH
VMEM_LIMIT = 56 * 2**20
NT = (((1,), (1,)), ((), ()))
TN = (((0,), (0,)), ((), ()))
DMA = pltpu.SemaphoreType.DMA
BF16, F32 = jnp.bfloat16, jnp.float32


class Place:
    def __init__(self, n_row, n_col):
        self.n_row, self.n_col = n_row, n_col
        self.chips = n_row // 2
        self.side = math.isqrt(self.chips)
        self.row, self.col = lax.axis_index("row"), lax.axis_index("col")
        self.core = lax.rem(self.row, 2)
        chip = lax.div(self.row, 2)
        self.x, self.y = lax.div(chip, self.side), lax.rem(chip, self.side)

    def chip(self, k, sign=1):
        dx, dy = lax.div(k, self.side), lax.rem(k, self.side)
        x = lax.rem(self.x + sign * dx + self.side, self.side)
        y = lax.rem(self.y + sign * dy + self.side, self.side)
        return x * self.side + y

    def at(self, row=None, col=None):
        return (self.row if row is None else row, self.col if col is None else col)

    def sibling(self):
        return self.at(row=self.row + 1 - 2 * self.core)

    def peer_row(self, k):
        return lax.rem(self.row + k, self.n_row)

    def peer_col(self, k):
        return lax.rem(self.col + k + self.n_col, self.n_col)


def signal(barrier, device):
    pl.semaphore_signal(barrier, inc=1, device_id=device, device_id_type=MESH)


def remote(src, dst, send, recv, device):
    return pltpu.make_async_remote_copy(
        src_ref=src, dst_ref=dst, send_sem=send, recv_sem=recv, device_id=device, device_id_type=MESH
    )


def loop(start, stop, body):
    def step(i, carry):
        body(jnp.int32(i))
        return carry

    lax.fori_loop(start, stop, step, 0)


def lanes_of():
    return [(2 * way + half, 1 - 2 * way, half, way == half) for half in range(2) for way in range(2)]


def whole_kernel(
    n_row, n_col, scale,
    idx, mine, weight, cot, adj_hbm,
    output, gw, grad,
    adj, gathered, panels, part, chain, side, back, acc, terms, swapped, staged, arrived,
    g_local, g_swap, g_sum, g_arrived, z_buf,
    adj_sem, f_send, f_recv, n_send, n_recv, rc_send, rc_recv, rs_send, rs_recv, ac_send, ac_recv, as_send, as_recv,
    gx_send, gx_recv, gp_send, gp_recv, gz_send, gz_recv, go_send, go_recv, gy_send, gy_recv,
    x_send, x_recv, p_send, p_recv,
):
    at = Place(n_row, n_col)
    lanes = lanes_of()
    me, chips = at.col, at.chips
    my_chip = lax.div(at.row, 2)
    slots, size = adj_hbm.shape[0], adj_hbm.shape[1]
    blocks = acc.shape[0] * 2
    width = weight.shape[0]

    load_adj = pltpu.make_async_copy(adj_hbm, adj.at[pl.ds(0, slots)], adj_sem)
    load_adj.start()

    barrier = pltpu.get_barrier_semaphore()
    loop(1, chips, lambda k: signal(barrier, at.at(row=at.chip(k) * 2 + at.core)))
    signal(barrier, at.sibling())
    loop(1, n_col, lambda k: signal(barrier, at.at(col=at.peer_col(k))))
    adj[slots] = jnp.zeros((size, size), BF16)
    pl.semaphore_wait(barrier, chips + n_col - 1)

    def same_core(k):
        return at.at(row=at.chip(k) * 2 + at.core)

    def far(k):
        return remote(mine, gathered.at[at.row], f_send.at[k], f_recv.at[k], same_core(k))

    def near(k):
        held = gathered.at[at.chip(k, -1) * 2 + at.core]
        return remote(held, held, n_send.at[k], n_recv.at[k], at.sibling())

    loop(1, chips, lambda k: far(k).start())
    gathered[at.row] = mine[...]
    near(jnp.int32(0)).start()

    def pass_on(k):
        far(k).wait_recv()
        near(k).start()

    loop(1, chips, pass_on)
    load_adj.wait()
    loop(0, chips, lambda k: near(k).wait_recv())
    panels[...] = gathered[...].reshape(panels.shape)

    def row_of(r):
        return jnp.concatenate([adj[idx[r * blocks + c]] for c in range(blocks)], axis=1)

    def aggregate(a, b):
        both = jnp.concatenate([row_of(a), row_of(b)], axis=0)
        made = lax.dot_general(both, panels[...], NT, preferred_element_type=F32).astype(BF16)
        part[a] = made[:size]
        part[b] = made[size:]

    def aggregate_first(i):
        a = at.peer_col(8 - i)
        aggregate(a, at.peer_col(-7 * i))

    loop(0, 2, aggregate_first)

    half_rows = size // 2

    def piece(k, half):
        return part.at[at.peer_col(k), pl.ds(half * half_rows, half_rows)]

    def rc(lane, sign, t, src):
        return remote(src, chain.at[lane, t], rc_send.at[lane, t], rc_recv.at[lane, t], at.at(col=at.peer_col(2 * sign)))

    def rs(lane, sign, half, t):
        src = piece(sign * (7 - 2 * t), half)
        return remote(src, side.at[lane, t], rs_send.at[lane, t], rs_recv.at[lane, t], at.at(col=at.peer_col(sign)))

    for lane, sign, half, long in lanes:
        if long:
            rc(lane, sign, 0, piece(8 * sign, half)).start()
    for lane, sign, half, long in lanes:
        rs(lane, sign, half, 0).start()

    def rs_step(t):
        loop(0, 2, lambda i: aggregate(at.peer_col(8 - 2 * t - i), at.peer_col(2 * t + i - 8)))
        for lane, sign, half, long in lanes:
            total = piece(sign * (8 - 2 * t), half)[...].astype(F32)
            rs(lane, sign, half, t - 1).wait_recv()
            total += side[lane, t - 1].astype(F32)
            if long:
                rc(lane, sign, t - 1, chain.at[lane, t - 1]).wait_recv()
                total += chain[lane, t - 1].astype(F32)
                chain[lane, t - 1] = total.astype(BF16)
            else:

                @pl.when(t > 1)
                def _():
                    rc(lane, sign, t - 1, chain.at[lane, t - 1]).wait_recv()
                    chain[lane, t - 1] = (total + chain[lane, t - 1].astype(F32)).astype(BF16)

                @pl.when(t == 1)
                def _():
                    chain[lane, 0] = total.astype(BF16)

            rc(lane, sign, t, chain.at[lane, t - 1]).start()
            rs(lane, sign, half, t).start()

    loop(1, 4, rs_step)
    halves = [part[me, h * half_rows : (h + 1) * half_rows].astype(F32) for h in range(2)]
    for lane, sign, half, long in lanes:
        rs(lane, sign, half, 3).wait_recv()
        rc(lane, sign, 3, chain.at[lane, 3]).wait_recv()
        halves[half] += side[lane, 3].astype(F32) + chain[lane, 3].astype(F32)
    aggregated = jnp.concatenate(halves, axis=0).astype(BF16)

    preact = jnp.dot(aggregated, weight[...], preferred_element_type=F32)
    sigmoid = jax.nn.sigmoid(preact)
    slopes = sigmoid * (1.0 + preact * (1.0 - sigmoid))
    deltas = (cot[...].astype(F32) * slopes).astype(BF16)
    back[me] = lax.dot_general(weight[...], deltas, NT, preferred_element_type=F32).astype(BF16)

    half_back = width // 2

    def held(k, half):
        return back.at[at.peer_col(k), pl.ds(half * half_back, half_back)]

    def ac(lane, sign, half, t):
        ref = held(-2 * sign * t, half)
        return remote(ref, ref, ac_send.at[lane, t], ac_recv.at[lane, t], at.at(col=at.peer_col(2 * sign)))

    def ac_wait(lane, sign, half, t):
        ref = held(-2 * sign * (t + 1), half)
        remote(ref, ref, ac_send.at[lane, t], ac_recv.at[lane, t], at.at(col=at.peer_col(2 * sign))).wait_recv()

    def as_(lane, sign, half, t):
        ref = held(-2 * sign * t, half)
        return remote(ref, ref, as_send.at[lane, t], as_recv.at[lane, t], at.at(col=at.peer_col(sign)))

    def as_wait(lane, sign, half, t):
        ref = held(-sign * (2 * t + 1), half)
        remote(ref, ref, as_send.at[lane, t], as_recv.at[lane, t], at.at(col=at.peer_col(sign))).wait_recv()

    for lane, sign, half, long in lanes:
        ac(lane, sign, half, 0).start()
    for lane, sign, half, long in lanes:
        as_(lane, sign, half, 0).start()

    def columns(rows, q):
        return jnp.concatenate(
            [jnp.concatenate([adj[idx[r * blocks + 2 * q + i]] for i in range(2)], axis=1) for r in rows], axis=0
        )

    def spread(rows):
        lhs = jnp.concatenate([back[r] for r in rows], axis=1)
        return lambda q: jnp.dot(lhs, columns(rows, q), preferred_element_type=F32)

    output[...] = (preact * sigmoid).astype(BF16)
    g_local[...] = lax.dot_general(aggregated, deltas, TN, preferred_element_type=F32).reshape(g_local.shape)
    g_x = remote(g_local.at[:, 1 - at.core], g_swap, gx_send, gx_recv, at.sibling())
    g_x.start()
    own = spread([me])
    for q in range(blocks // 2):
        acc[q] = own(q)

    def g_p(k):
        return remote(g_sum.at[at.chip(k)], g_arrived.at[k - 1], gp_send.at[k], gp_recv, same_core(k))

    g_x.wait_recv()
    g_sum[...] = g_local[:, at.core] + g_swap[...]
    loop(1, chips, lambda k: g_p(k).start())

    def ag_step(t):
        for lane, sign, half, long in lanes:
            ac_wait(lane, sign, half, t - 1)
            if long:
                ac(lane, sign, half, t).start()
            else:
                pl.when(t < 3)(lambda: ac(lane, sign, half, t).start())
            as_(lane, sign, half, t).start()
        for lane, sign, half, long in lanes:
            as_wait(lane, sign, half, t - 1)

        def pair(i):
            k = 2 * t - 1 + i
            made = spread([at.peer_col(k), at.peer_col(-k)])
            for q in range(blocks // 2):
                acc[q] += made(q)

        loop(0, 2, pair)

    loop(1, 4, ag_step)

    if chips > 1:
        remote(g_arrived, g_arrived, gp_send.at[0], gp_recv, at.sibling()).wait_recv()
    total = g_sum[my_chip]
    for k in range(chips - 1):
        total += g_arrived[k]
    z_buf[me] = total

    def g_z(k):
        return remote(z_buf.at[me], z_buf.at[me], gz_send.at[k], gz_recv, at.at(col=at.peer_col(k)))

    loop(1, n_col, lambda k: g_z(k).start())

    for lane, sign, half, long in lanes:
        as_wait(lane, sign, half, 3)
    for lane, sign, half, long in lanes:
        if long:
            ac_wait(lane, sign, half, 3)

    nodes = terms.shape[3] // 2

    def swap(h):
        return remote(
            terms.at[:, 1 - at.core, :, pl.ds(h * nodes, nodes)], swapped.at[h], x_send.at[h], x_recv.at[h], at.sibling()
        )

    last = spread([at.peer_col(7), at.peer_col(-7), at.peer_col(8)])
    for q in range(blocks // 2):
        made = (acc[q] + last(q)).astype(BF16)
        terms[:, :, :, q * 2 * size : (q + 1) * 2 * size] = made.reshape(*terms.shape[:3], 2 * size)
        if (q + 1) % (blocks // 4) == 0:
            swap((q + 1) // (blocks // 4) - 1).start()

    def term(c, h):
        return terms[c, at.core, :, h * nodes : (h + 1) * nodes].astype(F32) + swapped[h, c].astype(F32)

    def plane(k, h):
        return remote(
            staged.at[h, at.chip(k)], arrived.at[h, k - 1], p_send.at[h, k], p_recv.at[h, k], same_core(k)
        )

    sums = []
    for h in range(2):
        swap(h).wait_recv()

        def add_and_send(k):
            staged[h, at.chip(k)] = term(at.chip(k), h).astype(BF16)
            plane(k, h).start()

        loop(1, chips, add_and_send)
        sums.append(term(my_chip, h))

    most = z_buf.at[pl.ds(0, n_col - 1)]
    remote(most, most, gz_send.at[0], gz_recv, at.sibling()).wait_recv()
    whole = z_buf[0]
    for k in range(1, n_col):
        whole += z_buf[k]
    gw[my_chip, at.core] = whole * scale

    def g_o(k):
        ref = gw.at[my_chip, at.core]
        return remote(ref, ref, go_send.at[k], go_recv, same_core(k))

    loop(1, chips, lambda k: g_o(k).start())
    if chips > 1:
        rest = gw.at[pl.ds(0, chips - 1), at.core]
        remote(rest, rest, go_send.at[0], go_recv, at.sibling()).wait_recv()
    g_y = remote(gw.at[:, at.core], gw.at[:, at.core], gy_send, gy_recv, at.sibling())
    g_y.start()

    for h in range(2):
        for k in range(1, chips):
            plane(jnp.int32(k), h).wait_recv()
            sums[h] += arrived[h, k - 1].astype(F32)
        grad[:, h * nodes : (h + 1) * nodes] = sums[h].astype(BF16)
    g_y.wait()

    g_x.wait_send()
    loop(0, chips, lambda k: near(k).wait_send())

    def drain(k):
        far(k).wait_send()
        g_p(k).wait_send()
        g_o(k).wait_send()
        for h in range(2):
            plane(k, h).wait_send()

    loop(1, chips, drain)
    loop(1, n_col, lambda k: g_z(k).wait_send())
    for h in range(2):
        swap(h).wait_send()

    for lane, sign, half, long in lanes:

        def drain_lane(t):
            rs(lane, sign, half, t).wait_send()
            as_(lane, sign, half, t).wait_send()

        loop(0, 4, drain_lane)
        loop(0 if long else 1, 4, lambda t: rc(lane, sign, t, chain.at[lane, t]).wait_send())
        loop(0, 4 if long else 3, lambda t: ac(lane, sign, half, t).wait_send())


def whole(idx, mine, weight, cot, adj, n_row, n_col, scale):
    some, nodes = mine.shape
    slots, size, _ = adj.shape
    width = weight.shape[0]
    chips = n_row // 2
    assert n_col == 16 and nodes % (2 * size) == 0
    vmem = pl.BlockSpec(memory_space=pltpu.VMEM)
    V = pltpu.VMEM
    few = max(chips - 1, 1)
    return pl.pallas_call(
        functools.partial(whole_kernel, n_row, n_col, scale),
        out_shape=(
            jax.ShapeDtypeStruct((size, width), BF16),
            jax.ShapeDtypeStruct((chips, 2, some, width), F32),
            jax.ShapeDtypeStruct((some, nodes), BF16),
        ),
        in_specs=[pl.BlockSpec(memory_space=pltpu.SMEM), vmem, vmem, vmem, pl.BlockSpec(memory_space=pl.ANY)],
        out_specs=(vmem,) * 3,
        scratch_shapes=[
            V((slots + 1, size, size), BF16),
            V((n_row, some, nodes), BF16),
            V((width, nodes), BF16),
            V((n_col, size, width), BF16),
            V((4, 4, size // 2, width), BF16),
            V((4, 4, size // 2, width), BF16),
            V((n_col, width, size), BF16),
            V((nodes // (2 * size), width, 2 * size), F32),
            V((chips, 2, some, nodes), BF16),
            V((2, chips, some, nodes // 2), BF16),
            V((2, chips, some, nodes // 2), BF16),
            V((2, few, some, nodes // 2), BF16),
            V((chips, 2, some, width), F32),
            V((chips, some, width), F32),
            V((chips, some, width), F32),
            V((few, some, width), F32),
            V((n_col, some, width), F32),
            DMA(()),
            *[DMA((chips,))] * 4,
            *[DMA((4, 4))] * 8,
            DMA(()), DMA(()),
            DMA((chips,)), DMA(()),
            DMA((n_col,)), DMA(()),
            DMA((chips,)), DMA(()),
            DMA(()), DMA(()),
            DMA((2,)), DMA((2,)),
            DMA((2, chips)), DMA((2, chips)),
        ],
        compiler_params=pltpu.CompilerParams(
            collective_id=0, has_side_effects=True, vmem_limit_bytes=VMEM_LIMIT
        ),
        name="whole",
    )(idx, mine, weight, cot, adj)


def block_table(rows, cols, count, n_rows, n_cols):
    slots = rows.shape[0]
    slot = jnp.arange(slots, dtype=jnp.int32)
    place = jnp.where(slot < count, rows * n_cols + cols, -1)
    here = place[:, None] == jnp.arange(n_rows * n_cols, dtype=jnp.int32)[None, :]
    return jnp.min(jnp.where(here, slot[:, None], slots), axis=0)


def solution(mesh):
    n_row, n_col = mesh.shape["row"], mesh.shape["col"]

    def shards(features, weight, adj_values, block_rows, block_cols, block_counts, cotangent):
        adj = adj_values[0, 0]
        nodes, width = features.shape[0], weight.shape[0]
        idx = block_table(block_rows[0, 0], block_cols[0, 0], block_counts[0, 0], n_col, nodes // adj.shape[1])
        scale = 1.0 / math.sqrt(nodes * n_col)
        output, gw, grad = whole(idx, features.T, weight, cotangent, adj, n_row, n_col, scale)
        return output, gw.reshape(width, width), grad.T

    return jax.shard_map(
        shards,
        mesh=mesh,
        in_specs=(
            P("col", "row"),
            P(),
            P("row", "col", None, None, None),
            P("row", "col", None),
            P("row", "col", None),
            P("row", "col"),
            P(("row", "col"), None),
        ),
        out_specs=(P(("row", "col"), None), P(), P("col", "row")),
        check_vma=False,
    )
```

```python
import functools
import math

import jax
import jax.numpy as jnp
from jax import lax
from jax.experimental import pallas as pl
from jax.experimental.pallas import tpu as pltpu
from jax.sharding import PartitionSpec as P

MESH = pl.DeviceIdType.MESH
VMEM_LIMIT = 56 * 2**20
NT = (((1,), (1,)), ((), ()))
TN = (((0,), (0,)), ((), ()))
DMA = pltpu.SemaphoreType.DMA
BF16, F32 = jnp.bfloat16, jnp.float32


class Place:
    def __init__(self, n_row, n_col):
        self.n_row, self.n_col = n_row, n_col
        self.chips = n_row // 2
        self.side = math.isqrt(self.chips)
        self.row, self.col = lax.axis_index("row"), lax.axis_index("col")
        self.core = lax.rem(self.row, 2)
        chip = lax.div(self.row, 2)
        self.x, self.y = lax.div(chip, self.side), lax.rem(chip, self.side)

    def chip(self, k, sign=1):
        dx, dy = lax.div(k, self.side), lax.rem(k, self.side)
        x = lax.rem(self.x + sign * dx + self.side, self.side)
        y = lax.rem(self.y + sign * dy + self.side, self.side)
        return x * self.side + y

    def at(self, row=None, col=None):
        return (self.row if row is None else row, self.col if col is None else col)

    def sibling(self):
        return self.at(row=self.row + 1 - 2 * self.core)

    def peer_row(self, k):
        return lax.rem(self.row + k, self.n_row)

    def peer_col(self, k):
        return lax.rem(self.col + k + self.n_col, self.n_col)


def signal(barrier, device):
    pl.semaphore_signal(barrier, inc=1, device_id=device, device_id_type=MESH)


def remote(src, dst, send, recv, device):
    return pltpu.make_async_remote_copy(
        src_ref=src, dst_ref=dst, send_sem=send, recv_sem=recv, device_id=device, device_id_type=MESH
    )


def loop(start, stop, body):
    def step(i, carry):
        body(jnp.int32(i))
        return carry

    lax.fori_loop(start, stop, step, 0)


def lanes_of():
    return [(2 * way + half, 1 - 2 * way, half, way == half) for half in range(2) for way in range(2)]


def whole_kernel(
    n_row, n_col, scale,
    rows, cols, count, mine, weight_hbm, cot_hbm, adj_hbm,
    output, gw, grad,
    table, idx, weight, cot, adj, gathered, panels, part, chain, side, back, acc, terms, swapped, staged, arrived,
    g_local, g_swap, g_sum, g_arrived, z_near, z_far,
    table_sem, weight_sem, cot_sem, adj_sem, f_send, f_recv, n_send, n_recv, rc_send, rc_recv, rs_send, rs_recv, ac_send, ac_recv, as_send, as_recv,
    gx_send, gx_recv, gp_send, gp_recv, gz_send, gz_recv, gf_send, gf_recv, go_send, go_recv, gy_send, gy_recv,
    x_send, x_recv, p_send, p_recv,
):
    at = Place(n_row, n_col)
    lanes = lanes_of()
    me, chips = at.col, at.chips
    my_chip = lax.div(at.row, 2)
    slots, size = adj_hbm.shape[0], adj_hbm.shape[1]
    blocks = acc.shape[0] * 2
    width = weight.shape[0]

    load_adj = pltpu.make_async_copy(adj_hbm, adj.at[pl.ds(0, slots)], adj_sem)
    load_weight = pltpu.make_async_copy(weight_hbm, weight, weight_sem)
    load_cot = pltpu.make_async_copy(cot_hbm, cot, cot_sem)
    load_adj.start()
    load_weight.start()
    load_cot.start()

    barrier = pltpu.get_barrier_semaphore()
    loop(1, chips, lambda k: signal(barrier, at.at(row=at.chip(k) * 2 + at.core)))
    signal(barrier, at.sibling())
    loop(1, n_col, lambda k: signal(barrier, at.at(col=at.peer_col(k))))
    adj[slots] = jnp.zeros((size, size), BF16)

    lanes_wide = table.shape[1]
    position = lax.broadcasted_iota(jnp.int32, table.shape, 0) * lanes_wide + lax.broadcasted_iota(jnp.int32, table.shape, 1)
    live = count[0]

    def note_slot(s, held):
        place = jnp.where(s < live, rows[s] * blocks + cols[s], -1)
        return jnp.where(position == place, s, held)

    table[...] = lax.fori_loop(0, slots, note_slot, jnp.full(table.shape, slots, jnp.int32))
    load_table = pltpu.make_async_copy(table, idx, table_sem)
    load_table.start()
    pl.semaphore_wait(barrier, chips + n_col - 1)

    def same_core(k):
        return at.at(row=at.chip(k) * 2 + at.core)

    def far(k):
        return remote(mine, gathered.at[at.row], f_send.at[k], f_recv.at[k], same_core(k))

    def near(k):
        held = gathered.at[at.chip(k, -1) * 2 + at.core]
        return remote(held, held, n_send.at[k], n_recv.at[k], at.sibling())

    loop(1, chips, lambda k: far(k).start())
    gathered[at.row] = mine[...]
    near(jnp.int32(0)).start()

    def pass_on(k):
        far(k).wait_recv()
        near(k).start()

    loop(1, chips, pass_on)
    load_adj.wait()
    load_table.wait()
    loop(0, chips, lambda k: near(k).wait_recv())
    panels[...] = gathered[...].reshape(panels.shape)

    per_line = lanes_wide // blocks

    def block(r, c):
        return adj[idx[lax.div(r, per_line), lax.rem(r, per_line) * blocks + c]]

    def row_of(r):
        return jnp.concatenate([block(r, c) for c in range(blocks)], axis=1)

    def aggregate(a, b):
        both = jnp.concatenate([row_of(a), row_of(b)], axis=0)
        made = lax.dot_general(both, panels[...], NT, preferred_element_type=F32).astype(BF16)
        part[a] = made[:size]
        part[b] = made[size:]

    half_rows = size // 2

    def piece(k, half):
        return part.at[at.peer_col(k), pl.ds(half * half_rows, half_rows)]

    def rc(lane, sign, t, src):
        return remote(src, chain.at[lane, t], rc_send.at[lane, t], rc_recv.at[lane, t], at.at(col=at.peer_col(2 * sign)))

    def rs(lane, sign, half, t):
        src = piece(sign * (7 - 2 * t), half)
        return remote(src, side.at[lane, t], rs_send.at[lane, t], rs_recv.at[lane, t], at.at(col=at.peer_col(sign)))

    def first(i):
        aggregate(at.peer_col(8 - i), at.peer_col(-7 * i))

        @pl.when(i == 0)
        def _():
            for lane, sign, half, long in lanes:
                if long:
                    rc(lane, sign, 0, piece(8 * sign, half)).start()

        @pl.when(i == 1)
        def _():
            for lane, sign, half, long in lanes:
                rs(lane, sign, half, 0).start()

    loop(0, 2, first)

    def rs_step(t):
        loop(0, 2, lambda i: aggregate(at.peer_col(8 - 2 * t - i), at.peer_col(2 * t + i - 8)))
        for lane, sign, half, long in lanes:
            total = piece(sign * (8 - 2 * t), half)[...].astype(F32)
            rs(lane, sign, half, t - 1).wait_recv()
            total += side[lane, t - 1].astype(F32)
            if long:
                rc(lane, sign, t - 1, chain.at[lane, t - 1]).wait_recv()
                total += chain[lane, t - 1].astype(F32)
                chain[lane, t - 1] = total.astype(BF16)
            else:

                @pl.when(t > 1)
                def _():
                    rc(lane, sign, t - 1, chain.at[lane, t - 1]).wait_recv()
                    chain[lane, t - 1] = (total + chain[lane, t - 1].astype(F32)).astype(BF16)

                @pl.when(t == 1)
                def _():
                    chain[lane, 0] = total.astype(BF16)

            rc(lane, sign, t, chain.at[lane, t - 1]).start()
            rs(lane, sign, half, t).start()

    loop(1, 4, rs_step)
    halves = [part[me, h * half_rows : (h + 1) * half_rows].astype(F32) for h in range(2)]
    for lane, sign, half, long in lanes:
        rs(lane, sign, half, 3).wait_recv()
        rc(lane, sign, 3, chain.at[lane, 3]).wait_recv()
        halves[half] += side[lane, 3].astype(F32) + chain[lane, 3].astype(F32)
    aggregated = jnp.concatenate(halves, axis=0).astype(BF16)

    load_weight.wait()
    load_cot.wait()
    preact = jnp.dot(aggregated, weight[...], preferred_element_type=F32)
    sigmoid = jax.nn.sigmoid(preact)
    slopes = sigmoid * (1.0 + preact * (1.0 - sigmoid))
    deltas = (cot[...].astype(F32) * slopes).astype(BF16)
    back[me] = lax.dot_general(weight[...], deltas, NT, preferred_element_type=F32).astype(BF16)

    half_back = width // 2

    def held(k, half):
        return back.at[at.peer_col(k), pl.ds(half * half_back, half_back)]

    def ac(lane, sign, half, t):
        ref = held(-2 * sign * t, half)
        return remote(ref, ref, ac_send.at[lane, t], ac_recv.at[lane, t], at.at(col=at.peer_col(2 * sign)))

    def ac_wait(lane, sign, half, t):
        ref = held(-2 * sign * (t + 1), half)
        remote(ref, ref, ac_send.at[lane, t], ac_recv.at[lane, t], at.at(col=at.peer_col(2 * sign))).wait_recv()

    def as_(lane, sign, half, t):
        ref = held(-2 * sign * t, half)
        return remote(ref, ref, as_send.at[lane, t], as_recv.at[lane, t], at.at(col=at.peer_col(sign)))

    def as_wait(lane, sign, half, t):
        ref = held(-sign * (2 * t + 1), half)
        remote(ref, ref, as_send.at[lane, t], as_recv.at[lane, t], at.at(col=at.peer_col(sign))).wait_recv()

    for lane, sign, half, long in lanes:
        ac(lane, sign, half, 0).start()
    for lane, sign, half, long in lanes:
        as_(lane, sign, half, 0).start()

    def columns(rows, q):
        return jnp.concatenate(
            [jnp.concatenate([block(r, 2 * q + i) for i in range(2)], axis=1) for r in rows], axis=0
        )

    def spread(rows):
        lhs = jnp.concatenate([back[r] for r in rows], axis=1)
        return lambda q: jnp.dot(lhs, columns(rows, q), preferred_element_type=F32)

    output[...] = (preact * sigmoid).astype(BF16)
    g_local[...] = lax.dot_general(aggregated, deltas, TN, preferred_element_type=F32).reshape(g_local.shape)
    g_x = remote(g_local.at[:, 1 - at.core], g_swap, gx_send, gx_recv, at.sibling())
    g_x.start()
    own = spread([me])
    for q in range(blocks // 2):
        acc[q] = own(q)

    def g_p(k):
        return remote(g_sum.at[at.chip(k)], g_arrived.at[k - 1], gp_send.at[k], gp_recv, same_core(k))

    g_x.wait_recv()
    g_sum[...] = g_local[:, at.core] + g_swap[...]
    loop(1, chips, lambda k: g_p(k).start())

    group, place = lax.div(me, 4), lax.rem(me, 4)

    def z_peer(k):
        return at.at(col=group * 4 + lax.rem(place + k, 4))

    def far_peer(k):
        return at.at(col=lax.rem(group + k, 4) * 4 + place)

    def g_z(k):
        return remote(z_near.at[place], z_near.at[place], gz_send.at[k], gz_recv, z_peer(k))

    def g_f(k):
        return remote(z_far.at[group], z_far.at[group], gf_send.at[k], gf_recv, far_peer(k))

    def grad_weight_stage(t):
        if t == 2:
            if chips > 1:
                remote(g_arrived, g_arrived, gp_send.at[0], gp_recv, at.sibling()).wait_recv()
            total = g_sum[my_chip]
            for k in range(chips - 1):
                total += g_arrived[k]
            z_near[place] = total
            loop(1, 4, lambda k: g_z(k).start())
        if t == 3:
            three = z_near.at[pl.ds(0, 3)]
            remote(three, three, gz_send.at[0], gz_recv, at.sibling()).wait_recv()
            z_far[group] = (z_near[0] + z_near[1]) + (z_near[2] + z_near[3])
            loop(1, 4, lambda k: g_f(k).start())

    for t in range(1, 4):
        for lane, sign, half, long in lanes:
            ac_wait(lane, sign, half, t - 1)
            if long or t < 3:
                ac(lane, sign, half, t).start()
            as_(lane, sign, half, t).start()
        for lane, sign, half, long in lanes:
            as_wait(lane, sign, half, t - 1)
        grad_weight_stage(t)

        def pair(i):
            k = 2 * t - 1 + i
            made = spread([at.peer_col(k), at.peer_col(-k)])
            for q in range(blocks // 2):
                acc[q] += made(q)

        loop(0, 2, pair)

    for lane, sign, half, long in lanes:
        as_wait(lane, sign, half, 3)
    for lane, sign, half, long in lanes:
        if long:
            ac_wait(lane, sign, half, 3)

    nodes = terms.shape[3] // 2

    def swap(h):
        return remote(
            terms.at[:, 1 - at.core, :, pl.ds(h * nodes, nodes)], swapped.at[h], x_send.at[h], x_recv.at[h], at.sibling()
        )

    last = spread([at.peer_col(7), at.peer_col(-7), at.peer_col(8)])
    for q in range(blocks // 2):
        made = (acc[q] + last(q)).astype(BF16)
        terms[:, :, :, q * 2 * size : (q + 1) * 2 * size] = made.reshape(*terms.shape[:3], 2 * size)
        if (q + 1) % (blocks // 4) == 0:
            swap((q + 1) // (blocks // 4) - 1).start()

    def term(c, h):
        return terms[c, at.core, :, h * nodes : (h + 1) * nodes].astype(F32) + swapped[h, c].astype(F32)

    def plane(k, h):
        return remote(
            staged.at[h, at.chip(k)], arrived.at[h, k - 1], p_send.at[h, k], p_recv.at[h, k], same_core(k)
        )

    three = z_far.at[pl.ds(0, 3)]
    remote(three, three, gf_send.at[0], gf_recv, at.sibling()).wait_recv()
    gw[my_chip, at.core] = ((z_far[0] + z_far[1]) + (z_far[2] + z_far[3])) * scale

    def g_o(k):
        ref = gw.at[my_chip, at.core]
        return remote(ref, ref, go_send.at[k], go_recv, same_core(k))

    loop(1, chips, lambda k: g_o(k).start())

    sums = []
    for h in range(2):
        swap(h).wait_recv()

        def add_and_send(k):
            staged[h, at.chip(k)] = term(at.chip(k), h).astype(BF16)
            plane(k, h).start()

        loop(1, chips, add_and_send)
        sums.append(term(my_chip, h))

    if chips > 1:
        rest = gw.at[pl.ds(0, chips - 1), at.core]
        remote(rest, rest, go_send.at[0], go_recv, at.sibling()).wait_recv()
    g_y = remote(gw.at[:, at.core], gw.at[:, at.core], gy_send, gy_recv, at.sibling())
    g_y.start()

    for h in range(2):
        for k in range(1, chips):
            plane(jnp.int32(k), h).wait_recv()
            sums[h] += arrived[h, k - 1].astype(F32)
        grad[:, h * nodes : (h + 1) * nodes] = sums[h].astype(BF16)
    g_y.wait()

    g_x.wait_send()
    loop(0, chips, lambda k: near(k).wait_send())

    def drain(k):
        far(k).wait_send()
        g_p(k).wait_send()
        g_o(k).wait_send()
        for h in range(2):
            plane(k, h).wait_send()

    loop(1, chips, drain)
    loop(1, 4, lambda k: g_z(k).wait_send())
    loop(1, 4, lambda k: g_f(k).wait_send())
    for h in range(2):
        swap(h).wait_send()

    for lane, sign, half, long in lanes:

        def drain_lane(t):
            rs(lane, sign, half, t).wait_send()
            as_(lane, sign, half, t).wait_send()

        loop(0, 4, drain_lane)
        loop(0 if long else 1, 4, lambda t: rc(lane, sign, t, chain.at[lane, t]).wait_send())
        loop(0, 4 if long else 3, lambda t: ac(lane, sign, half, t).wait_send())


def whole(rows, cols, count, mine, weight, cot, adj, n_row, n_col, scale):
    some, nodes = mine.shape
    slots, size, _ = adj.shape
    width = weight.shape[0]
    chips = n_row // 2
    assert n_col == 16 and nodes % (2 * size) == 0
    smem, vmem, hbm = (pl.BlockSpec(memory_space=m) for m in (pltpu.SMEM, pltpu.VMEM, pl.ANY))
    table = (n_col * (nodes // size) // 128, 128)
    V = pltpu.VMEM
    few = max(chips - 1, 1)
    return pl.pallas_call(
        functools.partial(whole_kernel, n_row, n_col, scale),
        out_shape=(
            jax.ShapeDtypeStruct((size, width), BF16),
            jax.ShapeDtypeStruct((chips, 2, some, width), F32),
            jax.ShapeDtypeStruct((some, nodes), BF16),
        ),
        in_specs=[smem, smem, smem, vmem, hbm, hbm, hbm],
        out_specs=(vmem,) * 3,
        scratch_shapes=[
            V(table, jnp.int32),
            pltpu.SMEM(table, jnp.int32),
            V((width, width), BF16),
            V((size, width), BF16),
            V((slots + 1, size, size), BF16),
            V((n_row, some, nodes), BF16),
            V((width, nodes), BF16),
            V((n_col, size, width), BF16),
            V((4, 4, size // 2, width), BF16),
            V((4, 4, size // 2, width), BF16),
            V((n_col, width, size), BF16),
            V((nodes // (2 * size), width, 2 * size), F32),
            V((chips, 2, some, nodes), BF16),
            V((2, chips, some, nodes // 2), BF16),
            V((2, chips, some, nodes // 2), BF16),
            V((2, few, some, nodes // 2), BF16),
            V((chips, 2, some, width), F32),
            V((chips, some, width), F32),
            V((chips, some, width), F32),
            V((few, some, width), F32),
            V((4, some, width), F32),
            V((4, some, width), F32),
            *[DMA(())] * 4,
            *[DMA((chips,))] * 4,
            *[DMA((4, 4))] * 8,
            DMA(()), DMA(()),
            DMA((chips,)), DMA(()),
            DMA((4,)), DMA(()), DMA((4,)), DMA(()),
            DMA((chips,)), DMA(()),
            DMA(()), DMA(()),
            DMA((2,)), DMA((2,)),
            DMA((2, chips)), DMA((2, chips)),
        ],
        compiler_params=pltpu.CompilerParams(
            collective_id=0, has_side_effects=True, vmem_limit_bytes=VMEM_LIMIT
        ),
        name="whole",
    )(rows, cols, count, mine, weight, cot, adj)


def hand_on_kernel(*refs):
    n = len(refs) // 3
    copies = [pltpu.make_async_copy(refs[i], refs[n + i], refs[2 * n + i]) for i in range(n)]
    for copy in copies:
        copy.start()
    for copy in copies:
        copy.wait()


def hand_on(*arrays):
    hbm = pl.BlockSpec(memory_space=pl.ANY)
    return pl.pallas_call(
        hand_on_kernel,
        out_shape=tuple(jax.ShapeDtypeStruct(a.shape, a.dtype) for a in arrays),
        in_specs=[hbm] * len(arrays),
        out_specs=(hbm,) * len(arrays),
        scratch_shapes=[DMA(())] * len(arrays),
        compiler_params=pltpu.CompilerParams(vmem_limit_bytes=VMEM_LIMIT),
        name="hand_on",
    )(*arrays)


def solution(mesh):
    n_row, n_col = mesh.shape["row"], mesh.shape["col"]

    def shards(features, weight, adj_values, block_rows, block_cols, block_counts, cotangent):
        adj = adj_values[0, 0]
        nodes, width = features.shape[0], weight.shape[0]
        scale = 1.0 / math.sqrt(nodes * n_col)
        made = whole(
            block_rows[0, 0], block_cols[0, 0], block_counts[0], features.T, weight, cotangent, adj, n_row, n_col, scale
        )
        output, gw, grad = hand_on(*made)
        return output, gw.reshape(width, width), grad.T

    return jax.shard_map(
        shards,
        mesh=mesh,
        in_specs=(
            P("col", "row"),
            P(),
            P("row", "col", None, None, None),
            P("row", "col", None),
            P("row", "col", None),
            P("row", "col"),
            P(("row", "col"), None),
        ),
        out_specs=(P(("row", "col"), None), P(), P("col", "row")),
        check_vma=False,
    )
```

```python
import functools
import math

import jax
import jax.numpy as jnp
from jax import lax
from jax.experimental import pallas as pl
from jax.experimental.pallas import tpu as pltpu
from jax.sharding import PartitionSpec as P

MESH = pl.DeviceIdType.MESH
VMEM_LIMIT = 56 * 2**20
NT = (((1,), (1,)), ((), ()))
TN = (((0,), (0,)), ((), ()))
DMA = pltpu.SemaphoreType.DMA
BF16, F32 = jnp.bfloat16, jnp.float32


class Place:
    def __init__(self, n_row, n_col):
        self.n_row, self.n_col = n_row, n_col
        self.chips = n_row // 2
        self.side = math.isqrt(self.chips)
        self.row, self.col = lax.axis_index("row"), lax.axis_index("col")
        self.core = lax.rem(self.row, 2)
        chip = lax.div(self.row, 2)
        self.x, self.y = lax.div(chip, self.side), lax.rem(chip, self.side)

    def chip(self, k, sign=1):
        dx, dy = lax.div(k, self.side), lax.rem(k, self.side)
        x = lax.rem(self.x + sign * dx + self.side, self.side)
        y = lax.rem(self.y + sign * dy + self.side, self.side)
        return x * self.side + y

    def at(self, row=None, col=None):
        return (self.row if row is None else row, self.col if col is None else col)

    def sibling(self):
        return self.at(row=self.row + 1 - 2 * self.core)

    def peer_row(self, k):
        return lax.rem(self.row + k, self.n_row)

    def peer_col(self, k):
        return lax.rem(self.col + k + self.n_col, self.n_col)


def signal(barrier, device):
    pl.semaphore_signal(barrier, inc=1, device_id=device, device_id_type=MESH)


def remote(src, dst, send, recv, device):
    return pltpu.make_async_remote_copy(
        src_ref=src, dst_ref=dst, send_sem=send, recv_sem=recv, device_id=device, device_id_type=MESH
    )


def loop(start, stop, body):
    def step(i, carry):
        body(jnp.int32(i))
        return carry

    lax.fori_loop(start, stop, step, 0)


def lanes_of():
    return [(2 * way + half, 1 - 2 * way, half, way == half) for half in range(2) for way in range(2)]


def whole_kernel(
    n_row, n_col, scale,
    rows, cols, count, mine, weight_hbm, cot_hbm, adj_hbm,
    output, gw, grad,
    table, idx, weight, cot, adj, gathered, panels, part, chain, side, back, acc, terms, swapped, staged, arrived,
    g_local, g_swap, g_sum, g_arrived, z_near, z_far,
    table_sem, weight_sem, cot_sem, adj_sem, f_send, f_recv, n_send, n_recv, rc_send, rc_recv, rs_send, rs_recv, ac_send, ac_recv, as_send, as_recv,
    gx_send, gx_recv, gp_send, gp_recv, gz_send, gz_recv, gf_send, gf_recv, go_send, go_recv, gy_send, gy_recv,
    x_send, x_recv, p_send, p_recv,
):
    at = Place(n_row, n_col)
    lanes = lanes_of()
    me, chips = at.col, at.chips
    my_chip = lax.div(at.row, 2)
    slots, size = adj_hbm.shape[0], adj_hbm.shape[1]
    blocks = acc.shape[0] * 2
    width = weight.shape[0]

    load_adj = pltpu.make_async_copy(adj_hbm, adj.at[pl.ds(0, slots)], adj_sem)
    load_weight = pltpu.make_async_copy(weight_hbm, weight, weight_sem)
    load_cot = pltpu.make_async_copy(cot_hbm, cot, cot_sem)
    load_adj.start()
    load_weight.start()
    load_cot.start()

    barrier = pltpu.get_barrier_semaphore()
    loop(1, chips, lambda k: signal(barrier, at.at(row=at.chip(k) * 2 + at.core)))
    signal(barrier, at.sibling())
    loop(1, n_col, lambda k: signal(barrier, at.at(col=at.peer_col(k))))
    adj[slots] = jnp.zeros((size, size), BF16)

    lanes_wide = table.shape[1]
    position = lax.broadcasted_iota(jnp.int32, table.shape, 0) * lanes_wide + lax.broadcasted_iota(jnp.int32, table.shape, 1)
    live = count[0, 0]

    def note_slot(s, held):
        place = jnp.where(s < live, rows[s] * blocks + cols[s], -1)
        return jnp.where(position == place, s, held)

    table[...] = lax.fori_loop(0, slots, note_slot, jnp.full(table.shape, slots, jnp.int32))
    load_table = pltpu.make_async_copy(table, idx, table_sem)
    load_table.start()
    pl.semaphore_wait(barrier, chips + n_col - 1)

    def same_core(k):
        return at.at(row=at.chip(k) * 2 + at.core)

    def sent(ref, sem):
        remote(ref, ref, sem, sem, at.sibling()).wait_send()

    def far(k):
        return remote(mine, gathered.at[at.row], f_send, f_recv.at[k], same_core(k))

    def near(k):
        held = gathered.at[at.chip(k, -1) * 2 + at.core]
        return remote(held, held, n_send, n_recv.at[k], at.sibling())

    loop(1, chips, lambda k: far(k).start())
    gathered[at.row] = mine[...]
    near(jnp.int32(0)).start()

    def pass_on(k):
        far(k).wait_recv()
        near(k).start()

    loop(1, chips, pass_on)
    load_adj.wait()
    load_table.wait()
    loop(0, chips, lambda k: near(k).wait_recv())
    panels[...] = gathered[...].reshape(panels.shape)

    per_line = lanes_wide // blocks

    def block(r, c):
        return adj[idx[lax.div(r, per_line), lax.rem(r, per_line) * blocks + c]]

    def row_of(r):
        return jnp.concatenate([block(r, c) for c in range(blocks)], axis=1)

    def aggregate(a, b):
        both = jnp.concatenate([row_of(a), row_of(b)], axis=0)
        made = lax.dot_general(both, panels[...], NT, preferred_element_type=F32).astype(BF16)
        part[a] = made[:size]
        part[b] = made[size:]

    half_rows = size // 2

    def piece(k, half):
        return part.at[at.peer_col(k), pl.ds(half * half_rows, half_rows)]

    def rc(lane, sign, t, src):
        return remote(src, chain.at[lane, t], rc_send.at[lane, t], rc_recv.at[lane, t], at.at(col=at.peer_col(2 * sign)))

    def rs(lane, sign, half, t):
        src = piece(sign * (7 - 2 * t), half)
        return remote(src, side.at[lane, t], rs_send.at[lane, t], rs_recv.at[lane, t], at.at(col=at.peer_col(sign)))

    def first(i):
        aggregate(at.peer_col(8 - i), at.peer_col(-7 * i))

        @pl.when(i == 0)
        def _():
            for lane, sign, half, long in lanes:
                if long:
                    rc(lane, sign, 0, piece(8 * sign, half)).start()

        @pl.when(i == 1)
        def _():
            for lane, sign, half, long in lanes:
                rs(lane, sign, half, 0).start()

    loop(0, 2, first)

    sent(gathered.at[pl.ds(0, chips)], n_send)
    if chips > 1:
        sent(gathered.at[pl.ds(0, chips - 1)], f_send)

    def rs_step(t):
        loop(0, 2, lambda i: aggregate(at.peer_col(8 - 2 * t - i), at.peer_col(2 * t + i - 8)))
        for lane, sign, half, long in lanes:
            total = piece(sign * (8 - 2 * t), half)[...].astype(F32)
            rs(lane, sign, half, t - 1).wait_recv()
            total += side[lane, t - 1].astype(F32)
            if long:
                rc(lane, sign, t - 1, chain.at[lane, t - 1]).wait_recv()
                total += chain[lane, t - 1].astype(F32)
                chain[lane, t - 1] = total.astype(BF16)
            else:

                @pl.when(t > 1)
                def _():
                    rc(lane, sign, t - 1, chain.at[lane, t - 1]).wait_recv()
                    chain[lane, t - 1] = (total + chain[lane, t - 1].astype(F32)).astype(BF16)

                @pl.when(t == 1)
                def _():
                    chain[lane, 0] = total.astype(BF16)

            rc(lane, sign, t, chain.at[lane, t - 1]).start()
            rs(lane, sign, half, t).start()

    loop(1, 4, rs_step)
    halves = [part[me, h * half_rows : (h + 1) * half_rows].astype(F32) for h in range(2)]
    for lane, sign, half, long in lanes:
        rs(lane, sign, half, 3).wait_recv()
        rc(lane, sign, 3, chain.at[lane, 3]).wait_recv()
        halves[half] += side[lane, 3].astype(F32) + chain[lane, 3].astype(F32)
    aggregated = jnp.concatenate(halves, axis=0).astype(BF16)

    load_weight.wait()
    load_cot.wait()
    preact = jnp.dot(aggregated, weight[...], preferred_element_type=F32)
    sigmoid = jax.nn.sigmoid(preact)
    slopes = sigmoid * (1.0 + preact * (1.0 - sigmoid))
    deltas = (cot[...].astype(F32) * slopes).astype(BF16)
    back[me] = lax.dot_general(weight[...], deltas, NT, preferred_element_type=F32).astype(BF16)

    half_back = width // 2

    def held(k, half):
        return back.at[at.peer_col(k), pl.ds(half * half_back, half_back)]

    def ac(lane, sign, half, t):
        ref = held(-2 * sign * t, half)
        return remote(ref, ref, ac_send.at[lane, t], ac_recv.at[lane, t], at.at(col=at.peer_col(2 * sign)))

    def ac_wait(lane, sign, half, t):
        ref = held(-2 * sign * (t + 1), half)
        remote(ref, ref, ac_send.at[lane, t], ac_recv.at[lane, t], at.at(col=at.peer_col(2 * sign))).wait_recv()

    def as_(lane, sign, half, t):
        ref = held(-2 * sign * t, half)
        return remote(ref, ref, as_send.at[lane, t], as_recv.at[lane, t], at.at(col=at.peer_col(sign)))

    def as_wait(lane, sign, half, t):
        ref = held(-sign * (2 * t + 1), half)
        remote(ref, ref, as_send.at[lane, t], as_recv.at[lane, t], at.at(col=at.peer_col(sign))).wait_recv()

    for lane, sign, half, long in lanes:
        ac(lane, sign, half, 0).start()
    for lane, sign, half, long in lanes:
        as_(lane, sign, half, 0).start()

    def columns(rows, q):
        return jnp.concatenate(
            [jnp.concatenate([block(r, 2 * q + i) for i in range(2)], axis=1) for r in rows], axis=0
        )

    def spread(rows):
        lhs = jnp.concatenate([back[r] for r in rows], axis=1)
        return lambda q: jnp.dot(lhs, columns(rows, q), preferred_element_type=F32)

    output[...] = (preact * sigmoid).astype(BF16)
    g_local[...] = lax.dot_general(aggregated, deltas, TN, preferred_element_type=F32).reshape(g_local.shape)
    g_x = remote(g_local.at[:, 1 - at.core], g_swap, gx_send, gx_recv, at.sibling())
    g_x.start()
    own = spread([me])
    for q in range(blocks // 2):
        acc[q] = own(q)

    def g_p(k):
        return remote(g_sum.at[at.chip(k)], g_arrived.at[k - 1], gp_send, gp_recv, same_core(k))

    for lane, sign, half, long in lanes:
        loop(0, 4, lambda t: rs(lane, sign, half, t).wait_send())
        loop(0 if long else 1, 4, lambda t: rc(lane, sign, t, chain.at[lane, t]).wait_send())
    g_x.wait()
    g_sum[...] = g_local[:, at.core] + g_swap[...]
    loop(1, chips, lambda k: g_p(k).start())

    group, place = lax.div(me, 4), lax.rem(me, 4)

    def z_peer(k):
        return at.at(col=group * 4 + lax.rem(place + k, 4))

    def far_peer(k):
        return at.at(col=lax.rem(group + k, 4) * 4 + place)

    def g_z(k):
        return remote(z_near.at[place], z_near.at[place], gz_send.at[k], gz_recv, z_peer(k))

    def g_f(k):
        return remote(z_far.at[group], z_far.at[group], gf_send.at[k], gf_recv, far_peer(k))

    def grad_weight_stage(t):
        if t == 2:
            if chips > 1:
                remote(g_arrived, g_arrived, gp_send, gp_recv, at.sibling()).wait_recv()
            total = g_sum[my_chip]
            for k in range(chips - 1):
                total += g_arrived[k]
            z_near[place] = total
            loop(1, 4, lambda k: g_z(k).start())
        if t == 3:
            three = z_near.at[pl.ds(0, 3)]
            remote(three, three, gz_send.at[0], gz_recv, at.sibling()).wait_recv()
            z_far[group] = (z_near[0] + z_near[1]) + (z_near[2] + z_near[3])
            loop(1, 4, lambda k: g_f(k).start())

    for t in range(1, 4):
        for lane, sign, half, long in lanes:
            ac_wait(lane, sign, half, t - 1)
            if long or t < 3:
                ac(lane, sign, half, t).start()
            as_(lane, sign, half, t).start()
        for lane, sign, half, long in lanes:
            as_wait(lane, sign, half, t - 1)
        grad_weight_stage(t)

        def pair(i):
            k = 2 * t - 1 + i
            made = spread([at.peer_col(k), at.peer_col(-k)])
            for q in range(blocks // 2):
                acc[q] += made(q)

        loop(0, 2, pair)

    for lane, sign, half, long in lanes:
        as_wait(lane, sign, half, 3)
    for lane, sign, half, long in lanes:
        if long:
            ac_wait(lane, sign, half, 3)

    nodes = terms.shape[3] // 2

    def swap(h):
        return remote(
            terms.at[:, 1 - at.core, :, pl.ds(h * nodes, nodes)], swapped.at[h], x_send.at[h], x_recv.at[h], at.sibling()
        )

    last = spread([at.peer_col(7), at.peer_col(-7), at.peer_col(8)])
    for q in range(blocks // 2):
        made = (acc[q] + last(q)).astype(BF16)
        terms[:, :, :, q * 2 * size : (q + 1) * 2 * size] = made.reshape(*terms.shape[:3], 2 * size)
        if (q + 1) % (blocks // 4) == 0:
            swap((q + 1) // (blocks // 4) - 1).start()

    def term(c, h):
        return terms[c, at.core, :, h * nodes : (h + 1) * nodes].astype(F32) + swapped[h, c].astype(F32)

    def plane(k, h):
        return remote(
            staged.at[h, at.chip(k)], arrived.at[h, k - 1], p_send, p_recv.at[h, k], same_core(k)
        )

    three = z_far.at[pl.ds(0, 3)]
    remote(three, three, gf_send.at[0], gf_recv, at.sibling()).wait_recv()
    gw[my_chip, at.core] = ((z_far[0] + z_far[1]) + (z_far[2] + z_far[3])) * scale

    def g_o(k):
        ref = gw.at[my_chip, at.core]
        return remote(ref, ref, go_send, go_recv, same_core(k))

    loop(1, chips, lambda k: g_o(k).start())

    sums = []
    for h in range(2):
        swap(h).wait_recv()

        def add_and_send(k):
            staged[h, at.chip(k)] = term(at.chip(k), h).astype(BF16)
            plane(k, h).start()

        loop(1, chips, add_and_send)
        sums.append(term(my_chip, h))

    loop(1, 4, lambda k: g_z(k).wait_send())
    loop(1, 4, lambda k: g_f(k).wait_send())
    for h in range(2):
        swap(h).wait_send()
    for lane, sign, half, long in lanes:
        loop(0, 4, lambda t: as_(lane, sign, half, t).wait_send())
        loop(0, 4 if long else 3, lambda t: ac(lane, sign, half, t).wait_send())
    if chips > 1:
        sent(g_sum.at[pl.ds(0, chips - 1)], gp_send)
    if chips > 1:
        rest = gw.at[pl.ds(0, chips - 1), at.core]
        remote(rest, rest, go_send, go_recv, at.sibling()).wait_recv()
    g_y = remote(gw.at[:, at.core], gw.at[:, at.core], gy_send, gy_recv, at.sibling())
    g_y.start()
    for h in range(2):
        for k in range(1, chips):
            plane(jnp.int32(k), h).wait_recv()
            sums[h] += arrived[h, k - 1].astype(F32)
        grad[:, h * nodes : (h + 1) * nodes] = sums[h].astype(BF16)
    g_y.wait()

    if chips > 1:
        most = staged.at[:, pl.ds(0, chips - 1)]
        sent(most, p_send)
        sent(gw.at[pl.ds(0, chips - 1), at.core], go_send)


def whole(rows, cols, count, mine, weight, cot, adj, n_row, n_col, scale):
    some, nodes = mine.shape
    slots, size, _ = adj.shape
    width = weight.shape[0]
    chips = n_row // 2
    assert n_col == 16 and nodes % (2 * size) == 0
    smem, vmem, hbm = (pl.BlockSpec(memory_space=m) for m in (pltpu.SMEM, pltpu.VMEM, pl.ANY))
    table = (n_col * (nodes // size) // 128, 128)
    V = pltpu.VMEM
    few = max(chips - 1, 1)
    return pl.pallas_call(
        functools.partial(whole_kernel, n_row, n_col, scale),
        out_shape=(
            jax.ShapeDtypeStruct((size, width), BF16),
            jax.ShapeDtypeStruct((chips, 2, some, width), F32),
            jax.ShapeDtypeStruct((some, nodes), BF16),
        ),
        in_specs=[smem, smem, smem, vmem, hbm, hbm, hbm],
        out_specs=(vmem,) * 3,
        scratch_shapes=[
            V(table, jnp.int32),
            pltpu.SMEM(table, jnp.int32),
            V((width, width), BF16),
            V((size, width), BF16),
            V((slots + 1, size, size), BF16),
            V((n_row, some, nodes), BF16),
            V((width, nodes), BF16),
            V((n_col, size, width), BF16),
            V((4, 4, size // 2, width), BF16),
            V((4, 4, size // 2, width), BF16),
            V((n_col, width, size), BF16),
            V((nodes // (2 * size), width, 2 * size), F32),
            V((chips, 2, some, nodes), BF16),
            V((2, chips, some, nodes // 2), BF16),
            V((2, chips, some, nodes // 2), BF16),
            V((2, few, some, nodes // 2), BF16),
            V((chips, 2, some, width), F32),
            V((chips, some, width), F32),
            V((chips, some, width), F32),
            V((few, some, width), F32),
            V((4, some, width), F32),
            V((4, some, width), F32),
            *[DMA(())] * 4,
            DMA(()), DMA((chips,)), DMA(()), DMA((chips,)),
            *[DMA((4, 4))] * 8,
            DMA(()), DMA(()),
            DMA(()), DMA(()),
            DMA((4,)), DMA(()), DMA((4,)), DMA(()),
            DMA(()), DMA(()),
            DMA(()), DMA(()),
            DMA((2,)), DMA((2,)),
            DMA(()), DMA((2, chips)),
        ],
        compiler_params=pltpu.CompilerParams(
            collective_id=0, has_side_effects=True, vmem_limit_bytes=VMEM_LIMIT
        ),
        name="whole",
    )(rows, cols, count, mine, weight, cot, adj)


def hand_on_kernel(*refs):
    n = len(refs) // 2
    for source, target in zip(refs[:n], refs[n:]):
        target[...] = source[...]


def hand_on(*arrays):
    vmem = pl.BlockSpec(memory_space=pltpu.VMEM)
    return pl.pallas_call(
        hand_on_kernel,
        out_shape=tuple(jax.ShapeDtypeStruct(a.shape, a.dtype) for a in arrays),
        in_specs=[vmem] * len(arrays),
        out_specs=(vmem,) * len(arrays),
        compiler_params=pltpu.CompilerParams(vmem_limit_bytes=VMEM_LIMIT),
        name="hand_on",
    )(*arrays)


def solution(mesh):
    n_row, n_col = mesh.shape["row"], mesh.shape["col"]

    def shards(features, weight, adj_values, block_rows, block_cols, block_counts, cotangent):
        adj = adj_values[0, 0]
        nodes, width = features.shape[0], weight.shape[0]
        scale = 1.0 / math.sqrt(nodes * n_col)
        made = whole(
            block_rows[0, 0], block_cols[0, 0], block_counts, features.T, weight, cotangent, adj, n_row, n_col, scale
        )
        output, gw, grad = hand_on(*made)
        return output, gw.reshape(width, width), grad.T

    return jax.shard_map(
        shards,
        mesh=mesh,
        in_specs=(
            P("col", "row"),
            P(),
            P("row", "col", None, None, None),
            P("row", "col", None),
            P("row", "col", None),
            P("row", "col"),
            P(("row", "col"), None),
        ),
        out_specs=(P(("row", "col"), None), P(), P("col", "row")),
        check_vma=False,
    )
```

```python
import functools
import math

import jax
import jax.numpy as jnp
from jax import lax
from jax.experimental import pallas as pl
from jax.experimental.pallas import tpu as pltpu
from jax.sharding import PartitionSpec as P

MESH = pl.DeviceIdType.MESH
VMEM_LIMIT = 56 * 2**20
NT = (((1,), (1,)), ((), ()))
TN = (((0,), (0,)), ((), ()))
DMA = pltpu.SemaphoreType.DMA
BF16, F32 = jnp.bfloat16, jnp.float32


class Place:
    def __init__(self, n_row, n_col):
        self.n_row, self.n_col = n_row, n_col
        self.chips = n_row // 2
        self.side = math.isqrt(self.chips)
        self.row, self.col = lax.axis_index("row"), lax.axis_index("col")
        self.core = lax.rem(self.row, 2)
        chip = lax.div(self.row, 2)
        self.x, self.y = lax.div(chip, self.side), lax.rem(chip, self.side)

    def chip(self, k, sign=1):
        dx, dy = lax.div(k, self.side), lax.rem(k, self.side)
        x = lax.rem(self.x + sign * dx + self.side, self.side)
        y = lax.rem(self.y + sign * dy + self.side, self.side)
        return x * self.side + y

    def at(self, row=None, col=None):
        return (self.row if row is None else row, self.col if col is None else col)

    def sibling(self):
        return self.at(row=self.row + 1 - 2 * self.core)

    def peer_row(self, k):
        return lax.rem(self.row + k, self.n_row)

    def peer_col(self, k):
        return lax.rem(self.col + k + self.n_col, self.n_col)


def signal(barrier, device):
    pl.semaphore_signal(barrier, inc=1, device_id=device, device_id_type=MESH)


def remote(src, dst, send, recv, device):
    return pltpu.make_async_remote_copy(
        src_ref=src, dst_ref=dst, send_sem=send, recv_sem=recv, device_id=device, device_id_type=MESH
    )


def loop(start, stop, body):
    def step(i, carry):
        body(jnp.int32(i))
        return carry

    lax.fori_loop(start, stop, step, 0)


def lanes_of():
    return [(2 * way + half, 1 - 2 * way, half, way == half) for half in range(2) for way in range(2)]


def whole_kernel(
    n_row, n_col, scale,
    rows, cols, count, mine, weight_hbm, cot_hbm, adj_hbm,
    output, gw, grad,
    table, idx, weight, cot, adj, gathered, panels, part, chain, side, back, acc, terms, swapped, staged, arrived,
    g_local, g_swap, g_sum, g_arrived, z_near, z_far,
    table_sem, weight_sem, cot_sem, adj_sem, f_send, f_recv, n_send, n_recv, rc_send, rc_recv, rs_send, rs_recv, ac_send, ac_recv, as_send, as_recv,
    gx_send, gx_recv, gp_send, gp_recv, gz_send, gz_recv, gf_send, gf_recv, go_send, go_recv, gy_send, gy_recv,
    x_send, x_recv, p_send, p_recv,
):
    at = Place(n_row, n_col)
    lanes = lanes_of()
    me, chips = at.col, at.chips
    my_chip = lax.div(at.row, 2)
    slots, size = adj_hbm.shape[0], adj_hbm.shape[1]
    blocks = acc.shape[0] * 2
    width = weight.shape[0]

    load_adj = pltpu.make_async_copy(adj_hbm, adj.at[pl.ds(0, slots)], adj_sem)
    load_weight = pltpu.make_async_copy(weight_hbm, weight, weight_sem)
    load_cot = pltpu.make_async_copy(cot_hbm, cot, cot_sem)
    load_adj.start()
    load_weight.start()
    load_cot.start()

    barrier = pltpu.get_barrier_semaphore()
    loop(1, chips, lambda k: signal(barrier, at.at(row=at.chip(k) * 2 + at.core)))
    signal(barrier, at.sibling())
    loop(1, n_col, lambda k: signal(barrier, at.at(col=at.peer_col(k))))
    adj[slots] = jnp.zeros((size, size), BF16)

    lanes_wide = table.shape[1]
    position = lax.broadcasted_iota(jnp.int32, table.shape, 0) * lanes_wide + lax.broadcasted_iota(jnp.int32, table.shape, 1)
    live = count[0, 0]

    def note_slot(s, held):
        place = jnp.where(s < live, rows[s] * blocks + cols[s], -1)
        return jnp.where(position == place, s, held)

    table[...] = lax.fori_loop(0, slots, note_slot, jnp.full(table.shape, slots, jnp.int32))
    load_table = pltpu.make_async_copy(table, idx, table_sem)
    load_table.start()
    pl.semaphore_wait(barrier, chips + n_col - 1)

    def same_core(k):
        return at.at(row=at.chip(k) * 2 + at.core)

    def sent(ref, sem):
        remote(ref, ref, sem, sem, at.sibling()).wait_send()

    edge = at.side
    nodes = mine.shape[1] // 2
    distant = sorted(range(1, edge), key=lambda d: -min(d, edge - d))
    nearby = distant[::-1]

    def chip(h, a, b):
        dx, dy = (a, b) if h == 0 else (b, a)
        return lax.rem(at.x + dx + edge, edge) * edge + lax.rem(at.y + dy + edge, edge)

    def there(h, a, b):
        return at.at(row=chip(h, a, b) * 2 + at.core)

    def feature(h, a, b):
        return gathered.at[chip(h, a, b) * 2 + at.core, :, pl.ds(h * nodes, nodes)]

    def first(h, d):
        return remote(mine.at[:, pl.ds(h * nodes, nodes)], feature(h, 0, 0), f_send, f_recv.at[h, d, 0], there(h, d, 0))

    def second(h, e, d):
        source = feature(h, -e, 0) if e else mine.at[:, pl.ds(h * nodes, nodes)]
        return remote(source, feature(h, -e, 0), f_send, f_recv.at[h, e, d], there(h, 0, d))

    def near(h, e, d):
        return remote(feature(h, -e, -d), feature(h, -e, -d), n_send, n_recv, at.sibling())

    for d in distant:
        for h in range(2):
            first(h, d).start()
    gathered[at.row] = mine[...]
    for d in distant:
        for h in range(2):
            second(h, 0, d).start()
    for h in range(2):
        near(h, 0, 0).start()
    for e in nearby:
        for h in range(2):
            first(h, e).wait_recv()
            for d in distant:
                second(h, e, d).start()
            near(h, e, 0).start()
    for e in (0, *nearby):
        for d in nearby:
            for h in range(2):
                second(h, e, d).wait_recv()
                near(h, e, d).start()
    load_adj.wait()
    load_table.wait()
    every = gathered.at[pl.ds(0, chips)]
    remote(every, every, n_send, n_recv, at.sibling()).wait_recv()
    panels[...] = gathered[...].reshape(panels.shape)

    per_line = lanes_wide // blocks

    def block(r, c):
        return adj[idx[lax.div(r, per_line), lax.rem(r, per_line) * blocks + c]]

    def row_of(r):
        return jnp.concatenate([block(r, c) for c in range(blocks)], axis=1)

    def aggregate(a, b):
        both = jnp.concatenate([row_of(a), row_of(b)], axis=0)
        made = lax.dot_general(both, panels[...], NT, preferred_element_type=F32).astype(BF16)
        part[a] = made[:size]
        part[b] = made[size:]

    half_rows = size // 2

    def piece(k, half):
        return part.at[at.peer_col(k), pl.ds(half * half_rows, half_rows)]

    def rc(lane, sign, t, src):
        return remote(src, chain.at[lane, t], rc_send.at[lane, t], rc_recv.at[lane, t], at.at(col=at.peer_col(2 * sign)))

    def rs(lane, sign, half, t):
        src = piece(sign * (7 - 2 * t), half)
        return remote(src, side.at[lane, t], rs_send.at[lane, t], rs_recv.at[lane, t], at.at(col=at.peer_col(sign)))

    def begin(i):
        aggregate(at.peer_col(8 - i), at.peer_col(-7 * i))

        @pl.when(i == 0)
        def _():
            for lane, sign, half, long in lanes:
                if long:
                    rc(lane, sign, 0, piece(8 * sign, half)).start()

        @pl.when(i == 1)
        def _():
            for lane, sign, half, long in lanes:
                rs(lane, sign, half, 0).start()

    loop(0, 2, begin)

    sent(gathered.at[pl.ds(0, chips)], n_send)
    if chips > 1:
        sent(gathered.at[pl.ds(0, chips - 1)], f_send)

    def rs_step(t):
        loop(0, 2, lambda i: aggregate(at.peer_col(8 - 2 * t - i), at.peer_col(2 * t + i - 8)))
        for lane, sign, half, long in lanes:
            total = piece(sign * (8 - 2 * t), half)[...].astype(F32)
            rs(lane, sign, half, t - 1).wait_recv()
            total += side[lane, t - 1].astype(F32)
            if long:
                rc(lane, sign, t - 1, chain.at[lane, t - 1]).wait_recv()
                total += chain[lane, t - 1].astype(F32)
                chain[lane, t - 1] = total.astype(BF16)
            else:

                @pl.when(t > 1)
                def _():
                    rc(lane, sign, t - 1, chain.at[lane, t - 1]).wait_recv()
                    chain[lane, t - 1] = (total + chain[lane, t - 1].astype(F32)).astype(BF16)

                @pl.when(t == 1)
                def _():
                    chain[lane, 0] = total.astype(BF16)

            rc(lane, sign, t, chain.at[lane, t - 1]).start()
            rs(lane, sign, half, t).start()

    loop(1, 4, rs_step)
    halves = [part[me, h * half_rows : (h + 1) * half_rows].astype(F32) for h in range(2)]
    for lane, sign, half, long in lanes:
        rs(lane, sign, half, 3).wait_recv()
        rc(lane, sign, 3, chain.at[lane, 3]).wait_recv()
        halves[half] += side[lane, 3].astype(F32) + chain[lane, 3].astype(F32)
    aggregated = jnp.concatenate(halves, axis=0).astype(BF16)

    load_weight.wait()
    load_cot.wait()
    preact = jnp.dot(aggregated, weight[...], preferred_element_type=F32)
    sigmoid = jax.nn.sigmoid(preact)
    slopes = sigmoid * (1.0 + preact * (1.0 - sigmoid))
    deltas = (cot[...].astype(F32) * slopes).astype(BF16)
    back[me] = lax.dot_general(weight[...], deltas, NT, preferred_element_type=F32).astype(BF16)

    half_back = width // 2

    def held(k, half):
        return back.at[at.peer_col(k), pl.ds(half * half_back, half_back)]

    def ac(lane, sign, half, t):
        ref = held(-2 * sign * t, half)
        return remote(ref, ref, ac_send.at[lane, t], ac_recv.at[lane, t], at.at(col=at.peer_col(2 * sign)))

    def ac_wait(lane, sign, half, t):
        ref = held(-2 * sign * (t + 1), half)
        remote(ref, ref, ac_send.at[lane, t], ac_recv.at[lane, t], at.at(col=at.peer_col(2 * sign))).wait_recv()

    def as_(lane, sign, half, t):
        ref = held(-2 * sign * t, half)
        return remote(ref, ref, as_send.at[lane, t], as_recv.at[lane, t], at.at(col=at.peer_col(sign)))

    def as_wait(lane, sign, half, t):
        ref = held(-sign * (2 * t + 1), half)
        remote(ref, ref, as_send.at[lane, t], as_recv.at[lane, t], at.at(col=at.peer_col(sign))).wait_recv()

    for lane, sign, half, long in lanes:
        ac(lane, sign, half, 0).start()
    for lane, sign, half, long in lanes:
        as_(lane, sign, half, 0).start()

    def columns(rows, q):
        return jnp.concatenate(
            [jnp.concatenate([block(r, 2 * q + i) for i in range(2)], axis=1) for r in rows], axis=0
        )

    def spread(rows):
        lhs = jnp.concatenate([back[r] for r in rows], axis=1)
        return lambda q: jnp.dot(lhs, columns(rows, q), preferred_element_type=F32)

    output[...] = (preact * sigmoid).astype(BF16)
    g_local[...] = lax.dot_general(aggregated, deltas, TN, preferred_element_type=F32).reshape(g_local.shape)
    g_x = remote(g_local.at[:, 1 - at.core], g_swap, gx_send, gx_recv, at.sibling())
    g_x.start()
    own = spread([me])
    for q in range(blocks // 2):
        acc[q] = own(q)

    def g_p(k):
        return remote(g_sum.at[at.chip(k)], g_arrived.at[k - 1], gp_send, gp_recv, same_core(k))

    for lane, sign, half, long in lanes:
        loop(0, 4, lambda t: rs(lane, sign, half, t).wait_send())
        loop(0 if long else 1, 4, lambda t: rc(lane, sign, t, chain.at[lane, t]).wait_send())
    g_x.wait()
    g_sum[...] = g_local[:, at.core] + g_swap[...]
    loop(1, chips, lambda k: g_p(k).start())

    group, place = lax.div(me, 4), lax.rem(me, 4)

    def z_peer(k):
        return at.at(col=group * 4 + lax.rem(place + k, 4))

    def far_peer(k):
        return at.at(col=lax.rem(group + k, 4) * 4 + place)

    def g_z(k):
        return remote(z_near.at[place], z_near.at[place], gz_send.at[k], gz_recv, z_peer(k))

    def g_f(k):
        return remote(z_far.at[group], z_far.at[group], gf_send.at[k], gf_recv, far_peer(k))

    def grad_weight_stage(t):
        if t == 2:
            if chips > 1:
                remote(g_arrived, g_arrived, gp_send, gp_recv, at.sibling()).wait_recv()
            total = g_sum[my_chip]
            for k in range(chips - 1):
                total += g_arrived[k]
            z_near[place] = total
            loop(1, 4, lambda k: g_z(k).start())
        if t == 3:
            three = z_near.at[pl.ds(0, 3)]
            remote(three, three, gz_send.at[0], gz_recv, at.sibling()).wait_recv()
            z_far[group] = (z_near[0] + z_near[1]) + (z_near[2] + z_near[3])
            loop(1, 4, lambda k: g_f(k).start())

    for t in range(1, 4):
        for lane, sign, half, long in lanes:
            ac_wait(lane, sign, half, t - 1)
            if long or t < 3:
                ac(lane, sign, half, t).start()
            as_(lane, sign, half, t).start()
        for lane, sign, half, long in lanes:
            as_wait(lane, sign, half, t - 1)
        grad_weight_stage(t)

        def pair(i):
            k = 2 * t - 1 + i
            made = spread([at.peer_col(k), at.peer_col(-k)])
            for q in range(blocks // 2):
                acc[q] += made(q)

        loop(0, 2, pair)

    for lane, sign, half, long in lanes:
        as_wait(lane, sign, half, 3)
    for lane, sign, half, long in lanes:
        if long:
            ac_wait(lane, sign, half, 3)

    def swap(h):
        return remote(
            terms.at[:, 1 - at.core, :, pl.ds(h * nodes, nodes)], swapped.at[h], x_send.at[h], x_recv.at[h], at.sibling()
        )

    last = spread([at.peer_col(7), at.peer_col(-7), at.peer_col(8)])
    for q in range(blocks // 2):
        made = (acc[q] + last(q)).astype(BF16)
        terms[:, :, :, q * 2 * size : (q + 1) * 2 * size] = made.reshape(*terms.shape[:3], 2 * size)
        if (q + 1) % (blocks // 4) == 0:
            swap((q + 1) // (blocks // 4) - 1).start()

    def term(c, h):
        return terms[c, at.core, :, h * nodes : (h + 1) * nodes].astype(F32) + swapped[h, c].astype(F32)

    def along_first(h, d, b):
        slot = (d - 1) * edge + b
        return remote(staged.at[h, chip(h, d, b)], arrived.at[h, slot], p_send, p_recv.at[h, slot], there(h, d, 0))

    def along_second(h, b):
        slot = (edge - 1) * edge + b - 1
        return remote(staged.at[h, chip(h, 0, b)], arrived.at[h, slot], p_send, p_recv.at[h, slot], there(h, 0, b))

    three = z_far.at[pl.ds(0, 3)]
    remote(three, three, gf_send.at[0], gf_recv, at.sibling()).wait_recv()
    gw[my_chip, at.core] = ((z_far[0] + z_far[1]) + (z_far[2] + z_far[3])) * scale

    def g_o(k):
        ref = gw.at[my_chip, at.core]
        return remote(ref, ref, go_send, go_recv, same_core(k))

    loop(1, chips, lambda k: g_o(k).start())

    for h in range(2):
        swap(h).wait_recv()
        for b in (*distant, 0):
            for d in distant:
                staged[h, chip(h, d, b)] = term(chip(h, d, b), h).astype(BF16)
                along_first(h, d, b).start()

    def gathered_sum(h, b):
        total = term(chip(h, 0, b), h)
        for d in nearby:
            along_first(h, d, b).wait_recv()
            total += arrived[h, (d - 1) * edge + b].astype(F32)
        return total

    for b in distant:
        for h in range(2):
            staged[h, chip(h, 0, b)] = gathered_sum(h, b).astype(BF16)
            along_second(h, b).start()

    loop(1, 4, lambda k: g_z(k).wait_send())
    loop(1, 4, lambda k: g_f(k).wait_send())
    for h in range(2):
        swap(h).wait_send()
    for lane, sign, half, long in lanes:
        loop(0, 4, lambda t: as_(lane, sign, half, t).wait_send())
        loop(0, 4 if long else 3, lambda t: ac(lane, sign, half, t).wait_send())
    if chips > 1:
        sent(g_sum.at[pl.ds(0, chips - 1)], gp_send)
    if chips > 1:
        rest = gw.at[pl.ds(0, chips - 1), at.core]
        remote(rest, rest, go_send, go_recv, at.sibling()).wait_recv()
    g_y = remote(gw.at[:, at.core], gw.at[:, at.core], gy_send, gy_recv, at.sibling())
    g_y.start()
    for h in range(2):
        total = gathered_sum(h, 0)
        for b in nearby:
            along_second(h, b).wait_recv()
            total += arrived[h, (edge - 1) * edge + b - 1].astype(F32)
        grad[:, h * nodes : (h + 1) * nodes] = total.astype(BF16)
    g_y.wait()

    if chips > 1:
        most = staged.at[:, pl.ds(0, chips - 1)]
        sent(most, p_send)
        sent(gw.at[pl.ds(0, chips - 1), at.core], go_send)


def whole(rows, cols, count, mine, weight, cot, adj, n_row, n_col, scale):
    some, nodes = mine.shape
    slots, size, _ = adj.shape
    width = weight.shape[0]
    chips = n_row // 2
    side = math.isqrt(chips)
    assert n_col == 16 and nodes % (2 * size) == 0
    smem, vmem, hbm = (pl.BlockSpec(memory_space=m) for m in (pltpu.SMEM, pltpu.VMEM, pl.ANY))
    table = (n_col * (nodes // size) // 128, 128)
    V = pltpu.VMEM
    few = max(chips - 1, 1)
    return pl.pallas_call(
        functools.partial(whole_kernel, n_row, n_col, scale),
        out_shape=(
            jax.ShapeDtypeStruct((size, width), BF16),
            jax.ShapeDtypeStruct((chips, 2, some, width), F32),
            jax.ShapeDtypeStruct((some, nodes), BF16),
        ),
        in_specs=[smem, smem, smem, vmem, hbm, hbm, hbm],
        out_specs=(vmem,) * 3,
        scratch_shapes=[
            V(table, jnp.int32),
            pltpu.SMEM(table, jnp.int32),
            V((width, width), BF16),
            V((size, width), BF16),
            V((slots + 1, size, size), BF16),
            V((n_row, some, nodes), BF16),
            V((width, nodes), BF16),
            V((n_col, size, width), BF16),
            V((4, 4, size // 2, width), BF16),
            V((4, 4, size // 2, width), BF16),
            V((n_col, width, size), BF16),
            V((nodes // (2 * size), width, 2 * size), F32),
            V((chips, 2, some, nodes), BF16),
            V((2, chips, some, nodes // 2), BF16),
            V((2, chips, some, nodes // 2), BF16),
            V((2, few, some, nodes // 2), BF16),
            V((chips, 2, some, width), F32),
            V((chips, some, width), F32),
            V((chips, some, width), F32),
            V((few, some, width), F32),
            V((4, some, width), F32),
            V((4, some, width), F32),
            *[DMA(())] * 4,
            DMA(()), DMA((2, side, side)), DMA(()), DMA(()),
            *[DMA((4, 4))] * 8,
            DMA(()), DMA(()),
            DMA(()), DMA(()),
            DMA((4,)), DMA(()), DMA((4,)), DMA(()),
            DMA(()), DMA(()),
            DMA(()), DMA(()),
            DMA((2,)), DMA((2,)),
            DMA(()), DMA((2, chips)),
        ],
        compiler_params=pltpu.CompilerParams(
            collective_id=0, has_side_effects=True, vmem_limit_bytes=VMEM_LIMIT
        ),
        name="whole",
    )(rows, cols, count, mine, weight, cot, adj)


def hand_on_kernel(*refs):
    n = len(refs) // 2
    for source, target in zip(refs[:n], refs[n:]):
        target[...] = source[...]


def hand_on(*arrays):
    vmem = pl.BlockSpec(memory_space=pltpu.VMEM)
    return pl.pallas_call(
        hand_on_kernel,
        out_shape=tuple(jax.ShapeDtypeStruct(a.shape, a.dtype) for a in arrays),
        in_specs=[vmem] * len(arrays),
        out_specs=(vmem,) * len(arrays),
        compiler_params=pltpu.CompilerParams(vmem_limit_bytes=VMEM_LIMIT),
        name="hand_on",
    )(*arrays)


def solution(mesh):
    n_row, n_col = mesh.shape["row"], mesh.shape["col"]

    def shards(features, weight, adj_values, block_rows, block_cols, block_counts, cotangent):
        adj = adj_values[0, 0]
        nodes, width = features.shape[0], weight.shape[0]
        scale = 1.0 / math.sqrt(nodes * n_col)
        made = whole(
            block_rows[0, 0], block_cols[0, 0], block_counts, features.T, weight, cotangent, adj, n_row, n_col, scale
        )
        output, gw, grad = hand_on(*made)
        return output, gw.reshape(width, width), grad.T

    return jax.shard_map(
        shards,
        mesh=mesh,
        in_specs=(
            P("col", "row"),
            P(),
            P("row", "col", None, None, None),
            P("row", "col", None),
            P("row", "col", None),
            P("row", "col"),
            P(("row", "col"), None),
        ),
        out_specs=(P(("row", "col"), None), P(), P("col", "row")),
        check_vma=False,
    )
```

```python
import functools
import math

import jax
import jax.numpy as jnp
from jax import lax
from jax.experimental import pallas as pl
from jax.experimental.pallas import tpu as pltpu
from jax.sharding import PartitionSpec as P

MESH = pl.DeviceIdType.MESH
VMEM_LIMIT = 52 * 2**20
NT = (((1,), (1,)), ((), ()))
TN = (((0,), (0,)), ((), ()))
DMA = pltpu.SemaphoreType.DMA
BF16, F32 = jnp.bfloat16, jnp.float32


class Place:
    def __init__(self, n_row, n_col):
        self.n_row, self.n_col = n_row, n_col
        self.chips = n_row // 2
        self.side = math.isqrt(self.chips)
        self.row, self.col = lax.axis_index("row"), lax.axis_index("col")
        self.core = lax.rem(self.row, 2)
        chip = lax.div(self.row, 2)
        self.x, self.y = lax.div(chip, self.side), lax.rem(chip, self.side)

    def chip(self, k, sign=1):
        dx, dy = lax.div(k, self.side), lax.rem(k, self.side)
        x = lax.rem(self.x + sign * dx + self.side, self.side)
        y = lax.rem(self.y + sign * dy + self.side, self.side)
        return x * self.side + y

    def at(self, row=None, col=None):
        return (self.row if row is None else row, self.col if col is None else col)

    def sibling(self):
        return self.at(row=self.row + 1 - 2 * self.core)

    def peer_row(self, k):
        return lax.rem(self.row + k, self.n_row)

    def peer_col(self, k):
        return lax.rem(self.col + k + self.n_col, self.n_col)


def signal(barrier, device):
    pl.semaphore_signal(barrier, inc=1, device_id=device, device_id_type=MESH)


def remote(src, dst, send, recv, device):
    return pltpu.make_async_remote_copy(
        src_ref=src, dst_ref=dst, send_sem=send, recv_sem=recv, device_id=device, device_id_type=MESH
    )


def loop(start, stop, body):
    def step(i, carry):
        body(jnp.int32(i))
        return carry

    lax.fori_loop(start, stop, step, 0)


PIECES = 2


def lanes_of():
    return [
        (PIECES * way + piece, 1 - 2 * way, piece, way == piece % 2) for piece in range(PIECES) for way in range(2)
    ]


def whole_kernel(
    n_row, n_col, scale,
    rows_hbm, cols_hbm, count_hbm, mine, weight_hbm, cot_hbm, adj_hbm,
    output, gw, grad,
    rows, cols, count, table, idx, weight, cot, adj, gathered, panels, part, chain, side, back, acc, terms, swapped, staged, arrived,
    g_local, g_swap, g_sum, g_arrived, z_near, z_far,
    tile_sem, table_sem, weight_sem, cot_sem, adj_sem, f_send, f_recv, n_send, n_recv, rc_send, rc_recv, rs_send, rs_recv, ac_send, ac_recv, as_send, as_recv,
    gx_send, gx_recv, gp_send, gp_recv, gz_send, gz_recv, gf_send, gf_recv, go_send, go_recv, gy_send, gy_recv,
    x_send, x_recv, p_send, p_recv,
):
    at = Place(n_row, n_col)
    lanes = lanes_of()
    me, chips = at.col, at.chips
    my_chip = lax.div(at.row, 2)
    slots, size = adj_hbm.shape[0], adj_hbm.shape[1]
    blocks = acc.shape[0] * 2
    width = weight.shape[0]

    load_adj = pltpu.make_async_copy(adj_hbm, adj.at[pl.ds(0, slots)], adj_sem)
    load_weight = pltpu.make_async_copy(weight_hbm, weight, weight_sem)
    load_cot = pltpu.make_async_copy(cot_hbm, cot, cot_sem)
    tile = ((rows_hbm, rows), (cols_hbm, cols), (count_hbm, count))
    load_tile = [pltpu.make_async_copy(a, b, tile_sem.at[i]) for i, (a, b) in enumerate(tile)]
    for load in load_tile:
        load.start()
    load_adj.start()
    load_weight.start()
    load_cot.start()

    barrier = pltpu.get_barrier_semaphore()
    loop(1, chips, lambda k: signal(barrier, at.at(row=at.chip(k) * 2 + at.core)))
    signal(barrier, at.sibling())
    loop(1, n_col, lambda k: signal(barrier, at.at(col=at.peer_col(k))))
    adj[slots] = jnp.zeros((size, size), BF16)

    lanes_wide = table.shape[1]
    position = lax.broadcasted_iota(jnp.int32, table.shape, 0) * lanes_wide + lax.broadcasted_iota(jnp.int32, table.shape, 1)
    for load in load_tile:
        load.wait()
    live = count[0, 0]

    def note_slot(s, held):
        place = jnp.where(s < live, rows[0, s] * blocks + cols[0, s], -1)
        return jnp.where(position == place, s, held)

    table[...] = lax.fori_loop(0, slots, note_slot, jnp.full(table.shape, slots, jnp.int32))
    load_table = pltpu.make_async_copy(table, idx, table_sem)
    load_table.start()
    pl.semaphore_wait(barrier, chips + n_col - 1)

    def same_core(k):
        return at.at(row=at.chip(k) * 2 + at.core)

    def sent(ref, sem):
        remote(ref, ref, sem, sem, at.sibling()).wait_send()

    edge = at.side
    nodes = mine.shape[1] // 2
    distant = sorted(range(1, edge), key=lambda d: -min(d, edge - d))
    nearby = distant[::-1]

    def chip(h, a, b):
        dx, dy = (a, b) if h == 0 else (b, a)
        return lax.rem(at.x + dx + edge, edge) * edge + lax.rem(at.y + dy + edge, edge)

    def there(h, a, b):
        return at.at(row=chip(h, a, b) * 2 + at.core)

    def feature(h, a, b):
        return gathered.at[chip(h, a, b) * 2 + at.core, :, pl.ds(h * nodes, nodes)]

    def first(h, d):
        return remote(mine.at[:, pl.ds(h * nodes, nodes)], feature(h, 0, 0), f_send, f_recv.at[h, d, 0], there(h, d, 0))

    def second(h, e, d):
        source = feature(h, -e, 0) if e else mine.at[:, pl.ds(h * nodes, nodes)]
        return remote(source, feature(h, -e, 0), f_send, f_recv.at[h, e, d], there(h, 0, d))

    def near(h, e, d):
        return remote(feature(h, -e, -d), feature(h, -e, -d), n_send, n_recv, at.sibling())

    for d in distant:
        for h in range(2):
            first(h, d).start()
    gathered[at.row] = mine[...]
    for d in distant:
        for h in range(2):
            second(h, 0, d).start()
    for h in range(2):
        near(h, 0, 0).start()
    for e in nearby:
        for h in range(2):
            first(h, e).wait_recv()
            for d in distant:
                second(h, e, d).start()
            near(h, e, 0).start()
    for e in (0, *nearby):
        for d in nearby:
            for h in range(2):
                second(h, e, d).wait_recv()
                near(h, e, d).start()
    load_adj.wait()
    load_table.wait()
    every = gathered.at[pl.ds(0, chips)]
    remote(every, every, n_send, n_recv, at.sibling()).wait_recv()
    panels[...] = gathered[...].reshape(panels.shape)

    per_line = lanes_wide // blocks

    def block(r, c):
        return adj[idx[lax.div(r, per_line), lax.rem(r, per_line) * blocks + c]]

    def row_of(r):
        return jnp.concatenate([block(r, c) for c in range(blocks)], axis=1)

    def aggregate(a, b):
        both = jnp.concatenate([row_of(a), row_of(b)], axis=0)
        made = lax.dot_general(both, panels[...], NT, preferred_element_type=F32).astype(BF16)
        part[a] = made[:size]
        part[b] = made[size:]

    half_rows = size // PIECES

    def piece(k, half):
        return part.at[at.peer_col(k), pl.ds(half * half_rows, half_rows)]

    def rc(lane, sign, t, src):
        return remote(src, chain.at[lane, t], rc_send.at[lane, t], rc_recv.at[lane, t], at.at(col=at.peer_col(2 * sign)))

    def rs(lane, sign, half, t):
        src = piece(sign * (7 - 2 * t), half)
        return remote(src, side.at[lane, t], rs_send.at[lane, t], rs_recv.at[lane, t], at.at(col=at.peer_col(sign)))

    def begin(i):
        aggregate(at.peer_col(8 - i), at.peer_col(-7 * i))

        @pl.when(i == 0)
        def _():
            for lane, sign, half, long in lanes:
                if long:
                    rc(lane, sign, 0, piece(8 * sign, half)).start()

        @pl.when(i == 1)
        def _():
            for lane, sign, half, long in lanes:
                rs(lane, sign, half, 0).start()

    loop(0, 2, begin)

    sent(gathered.at[pl.ds(0, chips)], n_send)
    if chips > 1:
        sent(gathered.at[pl.ds(0, chips - 1)], f_send)

    def rs_step(t):
        loop(0, 2, lambda i: aggregate(at.peer_col(8 - 2 * t - i), at.peer_col(2 * t + i - 8)))
        for lane, sign, half, long in lanes:
            total = piece(sign * (8 - 2 * t), half)[...].astype(F32)
            rs(lane, sign, half, t - 1).wait_recv()
            total += side[lane, t - 1].astype(F32)
            if long:
                rc(lane, sign, t - 1, chain.at[lane, t - 1]).wait_recv()
                total += chain[lane, t - 1].astype(F32)
                chain[lane, t - 1] = total.astype(BF16)
            else:

                @pl.when(t > 1)
                def _():
                    rc(lane, sign, t - 1, chain.at[lane, t - 1]).wait_recv()
                    chain[lane, t - 1] = (total + chain[lane, t - 1].astype(F32)).astype(BF16)

                @pl.when(t == 1)
                def _():
                    chain[lane, 0] = total.astype(BF16)

            rc(lane, sign, t, chain.at[lane, t - 1]).start()
            rs(lane, sign, half, t).start()

    loop(1, 4, rs_step)
    halves = [part[me, h * half_rows : (h + 1) * half_rows].astype(F32) for h in range(PIECES)]
    for lane, sign, half, long in lanes:
        rs(lane, sign, half, 3).wait_recv()
        rc(lane, sign, 3, chain.at[lane, 3]).wait_recv()
        halves[half] += side[lane, 3].astype(F32) + chain[lane, 3].astype(F32)
    aggregated = jnp.concatenate(halves, axis=0).astype(BF16)

    load_weight.wait()
    load_cot.wait()
    preact = jnp.dot(aggregated, weight[...], preferred_element_type=F32)
    sigmoid = jax.nn.sigmoid(preact)
    slopes = sigmoid * (1.0 + preact * (1.0 - sigmoid))
    deltas = (cot[...].astype(F32) * slopes).astype(BF16)
    back[me] = lax.dot_general(weight[...], deltas, NT, preferred_element_type=F32).astype(BF16)

    half_back = width // PIECES

    def held(k, half):
        return back.at[at.peer_col(k), pl.ds(half * half_back, half_back)]

    def ac(lane, sign, half, t):
        ref = held(-2 * sign * t, half)
        return remote(ref, ref, ac_send.at[lane, t], ac_recv.at[lane, t], at.at(col=at.peer_col(2 * sign)))

    def ac_wait(lane, sign, half, t):
        ref = held(-2 * sign * (t + 1), half)
        remote(ref, ref, ac_send.at[lane, t], ac_recv.at[lane, t], at.at(col=at.peer_col(2 * sign))).wait_recv()

    def as_(lane, sign, half, t):
        ref = held(-2 * sign * t, half)
        return remote(ref, ref, as_send.at[lane, t], as_recv.at[lane, t], at.at(col=at.peer_col(sign)))

    def as_wait(lane, sign, half, t):
        ref = held(-sign * (2 * t + 1), half)
        remote(ref, ref, as_send.at[lane, t], as_recv.at[lane, t], at.at(col=at.peer_col(sign))).wait_recv()

    for lane, sign, half, long in lanes:
        ac(lane, sign, half, 0).start()
    for lane, sign, half, long in lanes:
        as_(lane, sign, half, 0).start()

    def columns(rows, q):
        return jnp.concatenate(
            [jnp.concatenate([block(r, 2 * q + i) for i in range(2)], axis=1) for r in rows], axis=0
        )

    def spread(rows):
        lhs = jnp.concatenate([back[r] for r in rows], axis=1)
        return lambda q: jnp.dot(lhs, columns(rows, q), preferred_element_type=F32)

    output[...] = (preact * sigmoid).astype(BF16)
    g_local[...] = lax.dot_general(aggregated, deltas, TN, preferred_element_type=F32).reshape(g_local.shape)
    g_x = remote(g_local.at[:, 1 - at.core], g_swap, gx_send, gx_recv, at.sibling())
    g_x.start()
    own = spread([me])
    for q in range(blocks // 2):
        acc[q] = own(q)

    def g_p(k):
        return remote(g_sum.at[at.chip(k)], g_arrived.at[k - 1], gp_send, gp_recv, same_core(k))

    for lane, sign, half, long in lanes:
        loop(0, 4, lambda t: rs(lane, sign, half, t).wait_send())
        loop(0 if long else 1, 4, lambda t: rc(lane, sign, t, chain.at[lane, t]).wait_send())
    g_x.wait()
    g_sum[...] = g_local[:, at.core] + g_swap[...]
    loop(1, chips, lambda k: g_p(k).start())

    group, place = lax.div(me, 4), lax.rem(me, 4)

    def z_peer(k):
        return at.at(col=group * 4 + lax.rem(place + k, 4))

    def far_peer(k):
        return at.at(col=lax.rem(group + k, 4) * 4 + place)

    def g_z(k):
        return remote(z_near.at[place], z_near.at[place], gz_send.at[k], gz_recv, z_peer(k))

    def g_f(k):
        return remote(z_far.at[group], z_far.at[group], gf_send.at[k], gf_recv, far_peer(k))

    def grad_weight_stage(t):
        if t == 2:
            if chips > 1:
                remote(g_arrived, g_arrived, gp_send, gp_recv, at.sibling()).wait_recv()
            total = g_sum[my_chip]
            for k in range(chips - 1):
                total += g_arrived[k]
            z_near[place] = total
            loop(1, 4, lambda k: g_z(k).start())
        if t == 3:
            three = z_near.at[pl.ds(0, 3)]
            remote(three, three, gz_send.at[0], gz_recv, at.sibling()).wait_recv()
            z_far[group] = (z_near[0] + z_near[1]) + (z_near[2] + z_near[3])
            loop(1, 4, lambda k: g_f(k).start())

    for t in range(1, 4):
        for lane, sign, half, long in lanes:
            ac_wait(lane, sign, half, t - 1)
            if long or t < 3:
                ac(lane, sign, half, t).start()
            as_(lane, sign, half, t).start()
        for lane, sign, half, long in lanes:
            as_wait(lane, sign, half, t - 1)
        grad_weight_stage(t)

        def pair(i):
            k = 2 * t - 1 + i
            made = spread([at.peer_col(k), at.peer_col(-k)])
            for q in range(blocks // 2):
                acc[q] += made(q)

        loop(0, 2, pair)

    for lane, sign, half, long in lanes:
        as_wait(lane, sign, half, 3)
    for lane, sign, half, long in lanes:
        if long:
            ac_wait(lane, sign, half, 3)

    quarter = nodes // 2

    def swap(p):
        there_to = swapped.at[p // 2, :, :, pl.ds(p % 2 * quarter, quarter)]
        source = terms.at[:, 1 - at.core, :, pl.ds(p * quarter, quarter)]
        return remote(source, there_to, x_send.at[p], x_recv.at[p], at.sibling())

    last = spread([at.peer_col(7), at.peer_col(-7), at.peer_col(8)])
    for q in range(blocks // 2):
        made = (acc[q] + last(q)).astype(BF16)
        terms[:, :, :, q * 2 * size : (q + 1) * 2 * size] = made.reshape(*terms.shape[:3], 2 * size)
        if (q + 1) % (blocks // 8) == 0:
            swap((q + 1) // (blocks // 8) - 1).start()

    def term(c, h):
        return terms[c, at.core, :, h * nodes : (h + 1) * nodes].astype(F32) + swapped[h, c].astype(F32)

    def along_first(h, d, b):
        slot = (d - 1) * edge + b
        return remote(staged.at[h, chip(h, d, b)], arrived.at[h, slot], p_send, p_recv.at[h, slot], there(h, d, 0))

    def along_second(h, b):
        slot = (edge - 1) * edge + b - 1
        return remote(staged.at[h, chip(h, 0, b)], arrived.at[h, slot], p_send, p_recv.at[h, slot], there(h, 0, b))

    def g_o(k):
        ref = gw.at[my_chip, at.core]
        return remote(ref, ref, go_send, go_recv, same_core(k))

    def grad_weight_out():
        three = z_far.at[pl.ds(0, 3)]
        remote(three, three, gf_send.at[0], gf_recv, at.sibling()).wait_recv()
        gw[my_chip, at.core] = ((z_far[0] + z_far[1]) + (z_far[2] + z_far[3])) * scale
        loop(1, chips, lambda k: g_o(k).start())

    for h in range(2):
        swap(2 * h).wait_recv()
        swap(2 * h + 1).wait_recv()
        for b in (*distant, 0):
            for d in distant:
                staged[h, chip(h, d, b)] = term(chip(h, d, b), h).astype(BF16)
                along_first(h, d, b).start()
        if h == 0:
            grad_weight_out()

    def gathered_sum(h, b):
        total = term(chip(h, 0, b), h)
        for d in nearby:
            along_first(h, d, b).wait_recv()
            total += arrived[h, (d - 1) * edge + b].astype(F32)
        return total

    for b in distant:
        for h in range(2):
            staged[h, chip(h, 0, b)] = gathered_sum(h, b).astype(BF16)
            along_second(h, b).start()

    loop(1, 4, lambda k: g_z(k).wait_send())
    loop(1, 4, lambda k: g_f(k).wait_send())
    for p in range(4):
        swap(p).wait_send()
    for lane, sign, half, long in lanes:
        loop(0, 4, lambda t: as_(lane, sign, half, t).wait_send())
        loop(0, 4 if long else 3, lambda t: ac(lane, sign, half, t).wait_send())
    if chips > 1:
        sent(g_sum.at[pl.ds(0, chips - 1)], gp_send)
    if chips > 1:
        rest = gw.at[pl.ds(0, chips - 1), at.core]
        remote(rest, rest, go_send, go_recv, at.sibling()).wait_recv()
    g_y = remote(gw.at[:, at.core], gw.at[:, at.core], gy_send, gy_recv, at.sibling())
    g_y.start()
    for h in range(2):
        total = gathered_sum(h, 0)
        for b in nearby:
            along_second(h, b).wait_recv()
            total += arrived[h, (edge - 1) * edge + b - 1].astype(F32)
        grad[:, h * nodes : (h + 1) * nodes] = total.astype(BF16)
    g_y.wait()

    if chips > 1:
        most = staged.at[:, pl.ds(0, chips - 1)]
        sent(most, p_send)
        sent(gw.at[pl.ds(0, chips - 1), at.core], go_send)


def whole(rows, cols, count, mine, weight, cot, adj, n_row, n_col, scale):
    some, nodes = mine.shape
    slots, size, _ = adj.shape
    width = weight.shape[0]
    chips = n_row // 2
    side = math.isqrt(chips)
    assert n_col == 16 and nodes % (2 * size) == 0
    vmem, hbm = (pl.BlockSpec(memory_space=m) for m in (pltpu.VMEM, pltpu.HBM))
    table = (n_col * (nodes // size) // 128, 128)
    V = pltpu.VMEM
    few = max(chips - 1, 1)
    return pl.pallas_call(
        functools.partial(whole_kernel, n_row, n_col, scale),
        out_shape=(
            jax.ShapeDtypeStruct((size, width), BF16),
            jax.ShapeDtypeStruct((chips, 2, some, width), F32),
            jax.ShapeDtypeStruct((some, nodes), BF16),
        ),
        in_specs=[hbm, hbm, hbm, vmem, hbm, hbm, hbm],
        out_specs=(vmem,) * 3,
        scratch_shapes=[
            pltpu.SMEM((1, slots), jnp.int32),
            pltpu.SMEM((1, slots), jnp.int32),
            pltpu.SMEM((1, 1), jnp.int32),
            V(table, jnp.int32),
            pltpu.SMEM(table, jnp.int32),
            V((width, width), BF16),
            V((size, width), BF16),
            V((slots + 1, size, size), BF16),
            V((n_row, some, nodes), BF16),
            V((width, nodes), BF16),
            V((n_col, size, width), BF16),
            V((2 * PIECES, 4, size // PIECES, width), BF16),
            V((2 * PIECES, 4, size // PIECES, width), BF16),
            V((n_col, width, size), BF16),
            V((nodes // (2 * size), width, 2 * size), F32),
            V((chips, 2, some, nodes), BF16),
            V((2, chips, some, nodes // 2), BF16),
            V((2, chips, some, nodes // 2), BF16),
            V((2, few, some, nodes // 2), BF16),
            V((chips, 2, some, width), F32),
            V((chips, some, width), F32),
            V((chips, some, width), F32),
            V((few, some, width), F32),
            V((4, some, width), F32),
            V((4, some, width), F32),
            DMA((3,)),
            *[DMA(())] * 4,
            DMA(()), DMA((2, side, side)), DMA(()), DMA(()),
            *[DMA((2 * PIECES, 4))] * 8,
            DMA(()), DMA(()),
            DMA(()), DMA(()),
            DMA((4,)), DMA(()), DMA((4,)), DMA(()),
            DMA(()), DMA(()),
            DMA(()), DMA(()),
            DMA((4,)), DMA((4,)),
            DMA(()), DMA((2, chips)),
        ],
        compiler_params=pltpu.CompilerParams(
            collective_id=0, has_side_effects=True, vmem_limit_bytes=VMEM_LIMIT
        ),
        name="whole",
    )(rows, cols, count, mine, weight, cot, adj)


def hand_on_kernel(*refs):
    n = len(refs) // 2
    for source, target in zip(refs[:n], refs[n:]):
        target[...] = source[...]


def hand_on(*arrays):
    vmem = pl.BlockSpec(memory_space=pltpu.VMEM)
    return pl.pallas_call(
        hand_on_kernel,
        out_shape=tuple(jax.ShapeDtypeStruct(a.shape, a.dtype) for a in arrays),
        in_specs=[vmem] * len(arrays),
        out_specs=(vmem,) * len(arrays),
        compiler_params=pltpu.CompilerParams(vmem_limit_bytes=4 * 2**20),
        name="hand_on",
    )(*arrays)


def solution(mesh):
    n_row, n_col = mesh.shape["row"], mesh.shape["col"]

    def shards(features, weight, adj_values, block_rows, block_cols, block_counts, cotangent):
        adj = adj_values[0, 0]
        nodes, width = features.shape[0], weight.shape[0]
        scale = 1.0 / math.sqrt(nodes * n_col)
        made = whole(
            block_rows[0], block_cols[0], block_counts, features.T, weight, cotangent, adj, n_row, n_col, scale
        )
        output, gw, grad = hand_on(*made)
        return output, gw.reshape(width, width), grad.T

    return jax.shard_map(
        shards,
        mesh=mesh,
        in_specs=(
            P("col", "row"),
            P(),
            P("row", "col", None, None, None),
            P("row", "col", None),
            P("row", "col", None),
            P("row", "col"),
            P(("row", "col"), None),
        ),
        out_specs=(P(("row", "col"), None), P(), P("col", "row")),
        check_vma=False,
    )
```
